32 devices in a mesh: group: 8 (over z, y), mp: 4 (over x, core).
Axes of the slice: x: 2, y: 2, z: 4, core: 2. Of those that a mesh axis runs over, the one named last changes fastest.
Arguments:
- observations: bfloat16 [1024, 512], P('group', 'mp'), may hold values from -6 to 6
- hidden_state: bfloat16 [512, 1024], P('group', 'mp'), may hold values from -0.8984375 to 0.8984375
- cell_state: bfloat16 [512, 1024], P('group', 'mp'), may hold values from -4 to 4
- arrival_order: int32 [512], replicated, may hold values from 0 to 511, as said below
- batch_counts: int32 [8], replicated, may hold values from 0 to 128, as said below
- input_weight: bfloat16 [512, 4, 1024], P(None, None, 'mp'), may hold values from -0.15625 to 0.15625
- state_weight: bfloat16 [1024, 4, 1024], P(None, None, 'mp'), may hold values from -0.15625 to 0.15625
- gate_bias: float32 [4, 1024], P(None, 'mp'), may hold values from -3 to 3
- head_weight: bfloat16 [1024, 2, 512], P(None, None, 'mp'), may hold values from -0.1875 to 0.1875
- head_bias: float32 [2, 512], P(None, 'mp'), may hold values from -3 to 3
- value_weight: bfloat16 [512, 1], P('mp'), may hold values from -0.25 to 0.25
- value_bias: float32 [1], replicated, may hold values from -3 to 3
- advantage_weight: bfloat16 [512, 18], P('mp'), may hold values from -0.25 to 0.25
- advantage_bias: float32 [18], replicated, may hold values from -3 to 3
Outputs:
- action_values: float32 [1024, 18], P('group')
- new_hidden: bfloat16 [512, 1024], P('group', 'mp')
- new_cell: bfloat16 [512, 1024], P('group', 'mp')
The draws below stay inside these ranges and needn't reach their ends.
Inputs may be any that keep to these rules, and one draw needn't show every extreme that they name: `arrival_order`: A permutation: each actor id once. Positions starts[b] to starts[b] + batch_counts[b] - 1 hold the actors of batch b, where starts is the running sum of batch_counts. Of the actors of one owner (ids k * 64 to (k + 1) * 64 - 1), at most 16 lie in one batch. `batch_counts`: sums to 512.
All inputs are finite; a program needn't handle non-finite values.
Results may differ from the reference program's by a relative error of at most 0.0019.
Values may be sent and summed in bfloat16 or wider, within the bound.
No kernel may reach another device: no remote copies, remote signals or barrier semaphores. Data moves between devices by JAX's collectives and lax.ppermute only.
A program may use at most 64 MiB of HBM per device.

```python
import jax
import jax.numpy as jnp

H = 1024
FEAT = 512
HEADH = 512
NACT = 18
ACT_DEV = 64
ACTORS = 512
BATCHES = 8
CAPB = 128
PEER = 16


def layout(key):
    base_key = jax.random.fold_in(key, 7)
    busiest = jax.random.randint(jax.random.fold_in(base_key, 1), (), 0, BATCHES)
    slot_total = BATCHES * PEER
    slot_batch = jnp.arange(slot_total, dtype=jnp.int32) // PEER

    def owner_pick(owner_key):
        slot_ranks = jax.random.permutation(jax.random.fold_in(owner_key, 2), slot_total).astype(jnp.int32)
        slot_ranks = jnp.where(slot_batch == busiest, slot_ranks - slot_total, slot_ranks)
        chosen = jnp.argsort(slot_ranks, stable=True)[:ACT_DEV]
        shuffle = jax.random.permutation(jax.random.fold_in(owner_key, 3), ACT_DEV)
        return slot_batch[chosen][shuffle]
    owner_keys = jax.random.split(jax.random.fold_in(base_key, 4), BATCHES)
    batch_of = jax.vmap(owner_pick)(owner_keys).reshape(ACTORS).astype(jnp.int32)
    tie_break = jax.random.permutation(jax.random.fold_in(base_key, 5), ACTORS).astype(jnp.int32)
    arrival = jnp.argsort(batch_of * ACTORS + tie_break, stable=True).astype(jnp.int32)
    tallies = jnp.sum((batch_of[None, :] == jnp.arange(BATCHES, dtype=jnp.int32)[:, None]).astype(jnp.int32), axis=1).astype(jnp.int32)
    return (arrival, tallies)


def draw_arrival_order(key, part):
    return layout(key)[0]


def draw_batch_counts(key, part):
    return layout(key)[1]


def shard_levels(own_key, shape, cuts, least, top_value):
    def one(dim, parts):
        draws = jax.random.uniform(jax.random.fold_in(jax.random.fold_in(own_key, 6), dim), (parts,), jnp.float32, least / len(cuts), top_value / len(cuts))
        return jnp.repeat(jnp.exp(draws), shape[dim] // parts).reshape((-1,) + (1,) * (len(shape) - dim - 1))

    factor_of = one(*cuts[0])
    for cut in cuts[1:]:
        factor_of = factor_of * one(*cut)
    return factor_of


def gaussian(rng, shape, width, bound, cuts=(), held_as=jnp.bfloat16):
    gain = shard_levels(rng, shape, cuts, -0.22, 0.18) if cuts else 1.0
    entries = jax.random.normal(rng, shape, jnp.float32) * width * gain
    return jnp.minimum(jnp.maximum(entries, -bound), bound).astype(held_as)


def setup_inputs(seed: int = 0) -> dict:
    arg_keys = jax.random.split(jax.random.key(seed), 15)
    observations = gaussian(arg_keys[0], (BATCHES * CAPB, FEAT), 1.0, 6.0, ((0, 8), (1, 4)))
    hidden_state = jnp.clip(jax.random.uniform(arg_keys[1], (ACTORS, H), jnp.float32, -0.8984375, 0.8984375) * shard_levels(arg_keys[1], (ACTORS, H), ((0, 8), (1, 4)), -0.4, 0.0), -0.8984375, 0.8984375).astype(jnp.bfloat16)
    cell_state = gaussian(arg_keys[2], (ACTORS, H), 1.0, 4.0, ((0, 8), (1, 4)))
    arrival_order = draw_arrival_order(jax.random.fold_in(arg_keys[14], 71), 0)
    batch_counts = draw_batch_counts(jax.random.fold_in(arg_keys[14], 71), 0)
    input_weight = gaussian(arg_keys[5], (FEAT, 4, H), (FEAT + H) ** -0.5, 0.15625, ((2, 4),))
    state_weight = gaussian(arg_keys[6], (H, 4, H), (FEAT + H) ** -0.5, 0.15625, ((2, 4),))
    gate_bias = gaussian(arg_keys[7], (4, H), 0.5, 3.0, ((1, 4),), jnp.float32)
    head_weight = gaussian(arg_keys[8], (H, 2, HEADH), H ** -0.5, 0.1875, ((2, 4),))
    head_bias = gaussian(arg_keys[9], (2, HEADH), 0.5, 3.0, ((1, 4),), jnp.float32)
    value_weight = gaussian(arg_keys[10], (HEADH, 1), HEADH ** -0.5, 0.25, ((0, 4),))
    value_bias = gaussian(arg_keys[11], (1,), 1.0, 3.0, (), jnp.float32)
    advantage_weight = gaussian(arg_keys[12], (HEADH, NACT), HEADH ** -0.5, 0.25, ((0, 4),))
    advantage_bias = gaussian(arg_keys[13], (NACT,), 1.0, 3.0, (), jnp.float32)
    return dict(observations=observations, hidden_state=hidden_state, cell_state=cell_state, arrival_order=arrival_order, batch_counts=batch_counts, input_weight=input_weight, state_weight=state_weight, gate_bias=gate_bias, head_weight=head_weight, head_bias=head_bias, value_weight=value_weight, value_bias=value_bias, advantage_weight=advantage_weight, advantage_bias=advantage_bias)


def reference(observations, hidden_state, cell_state, arrival_order, batch_counts, input_weight, state_weight, gate_bias, head_weight, head_bias, value_weight, value_bias, advantage_weight, advantage_bias):
    batch_ends = jnp.cumsum(batch_counts).astype(jnp.int32)
    batch_starts = (batch_ends - batch_counts).astype(jnp.int32)
    position = jnp.zeros((ACTORS,), jnp.int32).at[arrival_order].set(jnp.arange(ACTORS, dtype=jnp.int32))
    batch_index = jnp.sum((position[:, None] >= batch_ends[None, :]).astype(jnp.int32), axis=1).astype(jnp.int32)
    obs_row = (batch_index * CAPB + position - batch_starts[batch_index]).astype(jnp.int32)
    obs_rows = observations[obs_row]
    gate_values = jnp.dot(obs_rows, input_weight.reshape(FEAT, 4 * H), preferred_element_type=jnp.float32)
    gate_values = gate_values + jnp.dot(hidden_state, state_weight.reshape(H, 4 * H), preferred_element_type=jnp.float32)
    gate_values = gate_values.reshape(ACTORS, 4, H) + gate_bias[None]
    cell_next = jax.nn.sigmoid(gate_values[:, 1]) * cell_state.astype(jnp.float32) + jax.nn.sigmoid(gate_values[:, 0]) * jnp.tanh(gate_values[:, 2])
    hidden_next = (jax.nn.sigmoid(gate_values[:, 3]) * jnp.tanh(cell_next)).astype(jnp.bfloat16)
    stream = jnp.dot(hidden_next, head_weight.reshape(H, 2 * HEADH), preferred_element_type=jnp.float32)
    stream = jax.nn.relu(stream.reshape(ACTORS, 2, HEADH) + head_bias[None]).astype(jnp.bfloat16)
    value_sum = jnp.dot(stream[:, 0], value_weight, preferred_element_type=jnp.float32) + value_bias
    advantage_sum = jnp.dot(stream[:, 1], advantage_weight, preferred_element_type=jnp.float32) + advantage_bias
    slot_values = value_sum + advantage_sum - jnp.mean(advantage_sum, axis=1, keepdims=True)
    action_values = jnp.zeros((BATCHES * CAPB, NACT), jnp.float32).at[obs_row].set(slot_values)
    return action_values, hidden_next, cell_next.astype(jnp.bfloat16)
```

```python
import functools

import jax
import jax.numpy as jnp
from jax import lax
from jax.experimental import pallas as pl
from jax.experimental.pallas import tpu as pltpu
from jax.sharding import PartitionSpec as P

BF16 = jnp.bfloat16
F32 = jnp.float32
I32 = jnp.int32
EXACT = lax.Precision.HIGHEST
VMEM = pl.BlockSpec(memory_space=pltpu.VMEM)
SMEM = pl.BlockSpec(memory_space=pltpu.SMEM)


def iota(shape, axis):
    return lax.broadcasted_iota(I32, shape, axis)


def split(values, divisor):
    if divisor & (divisor - 1) == 0:
        quotient = lax.shift_right_logical(values, jnp.int32(divisor.bit_length() - 1))
    else:
        quotient = ((values.astype(F32) + 0.5) * (1.0 / divisor)).astype(I32)
    return quotient, values - quotient * divisor


def one_hot(mask):
    return jnp.where(mask, 1.0, 0.0).astype(BF16)


def dot(left, right, contract=((1,), (0,)), precision=None):
    return lax.dot_general(
        left, right, (contract, ((), ())), precision=precision, preferred_element_type=F32
    )


def route_kernel(mp, per_owner, counts_ref, order_ref, obs_ref, send_ref, base_ref, slot_ref):
    blocks, capacity = order_ref.shape
    batches = counts_ref.shape[0]
    per_pair = capacity // batches
    own = lax.axis_index("group")
    ends = []
    total = jnp.int32(0)
    start = jnp.int32(0)
    for batch in range(batches):
        start = jnp.where(own == batch, total, start)
        total = total + counts_ref[batch]
        ends.append(total)
    count = counts_ref[own]
    lanes = iota((1, capacity), 1)
    batch_ids = iota((batches, capacity), 0)
    earlier = one_hot(iota((capacity, capacity), 0) < iota((capacity, capacity), 1))

    block, shift = split(start, capacity)
    first = order_ref[pl.ds(jnp.minimum(block, blocks - 1), 1), :]
    second = order_ref[pl.ds(jnp.minimum(block + 1, blocks - 1), 1), :]
    turn = lax.rem(capacity - shift, capacity)
    merged = jnp.where(lanes >= shift, first, second)
    window = pltpu.roll(jnp.broadcast_to(merged, (8, capacity)), turn, 1)[0:1]
    owner, _ = split(window, per_owner)
    filled = lanes < count
    by_owner = one_hot((batch_ids == owner) & filled)
    ahead = dot(by_owner, earlier)
    rank = jnp.sum(by_owner.astype(F32) * ahead, axis=0, keepdims=True).astype(I32)
    row_ids, rank_ids = split(iota((mp * capacity, capacity), 0), per_pair)
    row_owner, _ = split(row_ids, mp)
    target = jnp.where(filled, owner * per_pair + rank, -1)
    send_ref[...] = dot(
        one_hot(row_owner * per_pair + rank_ids == target), obs_ref[...]
    ).astype(send_ref.dtype)
    slot_ref[0:1, :] = jnp.where(filled, owner, -1)
    slot_ref[1:2, :] = rank

    actors = iota((per_owner, capacity), 0) + own * per_owner
    carry = jnp.zeros((batches, 1), F32)
    base = jnp.zeros((per_owner, 1), F32)
    for index in range(blocks):
        ids = order_ref[index : index + 1, :]
        here = lanes + index * capacity
        batch = jnp.zeros((1, capacity), I32)
        for end in ends:
            batch = batch + jnp.where(here >= end, 1, 0)
        mine = (ids >= own * per_owner) & (ids < (own + 1) * per_owner)
        by_batch = one_hot((batch_ids == batch) & mine)
        ahead = dot(by_batch, earlier) + carry
        wide = by_batch.astype(F32)
        place = jnp.sum(wide * ahead, axis=0, keepdims=True)
        place = place + (batch * (mp * per_pair)).astype(F32)
        carry = carry + jnp.sum(wide, axis=1, keepdims=True)
        base = base + jnp.sum(jnp.where(ids == actors, place, 0.0), axis=1, keepdims=True)
    base_ref[...] = jnp.broadcast_to(base, base_ref.shape).astype(I32)


def cell_kernel(
    mp, per_pair, offsets, base_ref, rows_ref, hidden_refs, cell_ref, input_ref, state_ref, bias_ref,
    hidden_ref, next_ref,
):
    per_owner, units = cell_ref.shape
    features = rows_ref.shape[1]
    me = lax.axis_index("mp")
    base = base_ref[:, 0:1]
    columns = iota((per_owner, rows_ref.shape[0]), 1)
    picks = jnp.concatenate([one_hot(columns == base + part * per_pair) for part in range(mp)], axis=0)
    picked = dot(picks, rows_ref[...]).astype(BF16)
    gates = None
    for part in range(mp):
        term = dot(
            picked[part * per_owner : (part + 1) * per_owner],
            input_ref[part * features : (part + 1) * features, :],
        )
        gates = term if gates is None else gates + term
    for (ref, column), offset in zip(hidden_refs, offsets):
        rows = pl.ds(pl.multiple_of(jnp.bitwise_xor(me, offset) * units, units), units)
        gates = gates + dot(ref[:, column : column + units], state_ref[rows, :])
    gate = [
        gates[:, k * units : (k + 1) * units] + bias_ref[k : k + 1, :] for k in range(4)
    ]
    cell = jax.nn.sigmoid(gate[1]) * cell_ref[...].astype(F32) + jax.nn.sigmoid(gate[0]) * jnp.tanh(gate[2])
    next_ref[...] = cell.astype(BF16)
    hidden_ref[...] = (jax.nn.sigmoid(gate[3]) * jnp.tanh(cell)).astype(BF16)


def head_kernel(
    mp, per_pair, offsets, base_ref, hidden_refs, head_ref, head_bias_ref, value_ref, value_bias_ref,
    advantage_ref, advantage_bias_ref, send_ref,
):
    per_owner = base_ref.shape[0]
    units = head_ref.shape[0] // mp
    width = head_bias_ref.shape[1]
    actions = advantage_ref.shape[0]
    me = lax.axis_index("mp")
    total = None
    for (ref, column), offset in zip(hidden_refs, offsets):
        rows = pl.ds(pl.multiple_of(jnp.bitwise_xor(me, offset) * units, units), units)
        term = dot(ref[:, column : column + units], head_ref[rows, :])
        total = term if total is None else total + term
    value_stream = jnp.maximum(total[:, :width] + head_bias_ref[0:1, :], 0.0).astype(BF16)
    advantage_stream = jnp.maximum(total[:, width:] + head_bias_ref[1:2, :], 0.0).astype(BF16)
    value = jnp.sum(
        value_stream.astype(F32) * value_ref[...].astype(F32), axis=1, keepdims=True
    )
    advantage = dot(advantage_stream, advantage_ref[...], ((1,), (1,)))
    first = jnp.where(me == 0, 1.0, 0.0)
    advantage = advantage + advantage_bias_ref[...] * first
    value = value + value_bias_ref[0] * first
    mixed = value + advantage - jnp.sum(advantage, axis=1, keepdims=True) * (1.0 / actions)
    lanes = send_ref.shape[2]
    lane_rank, lane_action = split(iota((actions, lanes), 1), actions)
    spread = dot(
        mixed,
        jnp.where(
            (lane_action == iota((actions, lanes), 0)) & (lane_rank < per_pair), 1.0, 0.0
        ),
        precision=EXACT,
    )
    batch, rank = split(base_ref[:, 0:1], mp * per_pair)
    spread = jnp.where(split(iota((per_owner, lanes), 1), actions)[0] == rank, spread, 0.0)
    rows = send_ref.shape[0]
    to_row = jnp.where(split(iota((per_owner, rows), 1), mp)[0] == batch, 1.0, 0.0)
    send_ref[:, 0, :] = dot(to_row, spread, ((0,), (0,)), precision=EXACT)


def place_kernel(mp, per_pair, slot_ref, rows_ref, out_ref):
    actions, capacity = out_ref.shape
    rows, _, lanes = rows_ref.shape
    owner = slot_ref[0:1, :]
    rank = slot_ref[1:2, :]
    to_slot = jnp.where(split(iota((rows, capacity), 0), mp)[0] == owner, 1.0, 0.0)
    spread = dot(rows_ref[:, 0, :], to_slot, ((0,), (0,)), precision=EXACT)
    spread = jnp.where(split(iota((lanes, capacity), 0), actions)[0] == rank, spread, 0.0)
    lane_rank, lane_action = split(iota((actions, lanes), 1), actions)
    pick = jnp.where((lane_action == iota((actions, lanes), 0)) & (lane_rank < per_pair), 1.0, 0.0)
    out_ref[...] = dot(pick, spread, precision=EXACT)


def call(kernel, out_shape, specs, *args):
    return pl.pallas_call(
        kernel,
        out_shape=out_shape,
        in_specs=specs,
        out_specs=jax.tree.map(lambda _: VMEM, out_shape),
    )(*args)


def gather_parts(part, mp):
    arrays = [part]
    places = [(0, 0)]
    offsets = [0]
    width = part.shape[1]
    current = part
    distance = mp // 2
    while distance:
        pairs = [(device, device ^ distance) for device in range(mp)]
        got = lax.ppermute(current, "mp", pairs)
        places += [(len(arrays), k * width) for k in range(got.shape[1] // width)]
        arrays.append(got)
        offsets += [offset ^ distance for offset in offsets]
        distance //= 2
        if distance:
            current = jnp.concatenate([current, got], axis=1)
    return arrays, places, offsets


def per_device(
    observations,
    hidden_state,
    cell_state,
    arrival_order,
    batch_counts,
    input_weight,
    state_weight,
    gate_bias,
    head_weight,
    head_bias,
    value_weight,
    value_bias,
    advantage_weight,
    advantage_bias,
    *,
    mp,
):
    batches = batch_counts.shape[0]
    capacity, features = observations.shape
    per_owner, units = cell_state.shape
    per_pair = capacity // batches
    actions = advantage_weight.shape[1]
    rows = batches * mp
    everyone = ("group", "mp")

    hidden_arrays, hidden_places, offsets = gather_parts(hidden_state, mp)
    send, base, slot = call(
        functools.partial(route_kernel, mp, per_owner),
        (
            jax.ShapeDtypeStruct((rows * per_pair, features), BF16),
            jax.ShapeDtypeStruct((per_owner, 128), I32),
            jax.ShapeDtypeStruct((2, capacity), I32),
        ),
        [SMEM, VMEM, VMEM],
        batch_counts,
        arrival_order.reshape(-1, capacity),
        observations,
    )
    got = lax.all_to_all(send, everyone, 0, 0, tiled=True)

    count = len(hidden_arrays)

    def cell_body(base_ref, rows_ref, *refs):
        places = [(refs[array], column) for array, column in hidden_places]
        cell_kernel(mp, per_pair, offsets, base_ref, rows_ref, places, *refs[count:])

    new_hidden, new_cell = call(
        cell_body,
        (
            jax.ShapeDtypeStruct((per_owner, units), BF16),
            jax.ShapeDtypeStruct((per_owner, units), BF16),
        ),
        [VMEM] * (6 + count),
        base,
        got,
        *hidden_arrays,
        cell_state,
        input_weight.reshape(input_weight.shape[0], -1),
        state_weight.reshape(state_weight.shape[0], -1),
        gate_bias,
    )

    next_arrays, next_places, _ = gather_parts(new_hidden, mp)

    def head_body(base_ref, *refs):
        places = [(refs[array], column) for array, column in next_places]
        head_kernel(mp, per_pair, offsets, base_ref, places, *refs[count:])

    lanes = -(-per_pair * actions // 128) * 128
    values = call(
        head_body,
        jax.ShapeDtypeStruct((rows, 1, lanes), F32),
        [VMEM] * (4 + count) + [SMEM, VMEM, VMEM],
        base,
        *next_arrays,
        head_weight.reshape(head_weight.shape[0], -1),
        head_bias,
        value_weight.T,
        value_bias,
        advantage_weight.T,
        advantage_bias.reshape(1, -1),
    )
    back = lax.all_to_all(values, everyone, 0, 0, tiled=True)
    placed = call(
        functools.partial(place_kernel, mp, per_pair),
        jax.ShapeDtypeStruct((actions, capacity), F32),
        [VMEM, VMEM],
        slot,
        back,
    )
    return placed.T, new_hidden, new_cell


def solution(mesh):
    placed = (
        P("group", "mp"),
        P("group", "mp"),
        P("group", "mp"),
        P(),
        P(),
        P(None, None, "mp"),
        P(None, None, "mp"),
        P(None, "mp"),
        P(None, None, "mp"),
        P(None, "mp"),
        P("mp", None),
        P(),
        P("mp", None),
        P(),
    )
    return jax.shard_map(
        functools.partial(per_device, mp=mesh.shape["mp"]),
        mesh=mesh,
        in_specs=placed,
        out_specs=(P("group", None), P("group", "mp"), P("group", "mp")),
        check_vma=False,
    )
```

```python
import functools
import math

import jax
import jax.numpy as jnp
from jax import lax
from jax.experimental import pallas as pl
from jax.experimental.pallas import tpu as pltpu
from jax.sharding import PartitionSpec as P


BF16 = jnp.bfloat16
F32 = jnp.float32
I32 = jnp.int32
VMEM = pl.BlockSpec(memory_space=pltpu.VMEM)
HBM = pl.BlockSpec(memory_space=pltpu.HBM)


def iota(shape, axis):
    return lax.broadcasted_iota(I32, shape, axis)


def split(values, divisor):
    if divisor & (divisor - 1) == 0:
        quotient = lax.shift_right_logical(values, jnp.int32(divisor.bit_length() - 1))
    else:
        quotient = ((values.astype(F32) + 0.5) * (1.0 / divisor)).astype(I32)
    return quotient, values - quotient * divisor


def one_hot(mask):
    return jnp.where(mask, 1.0, 0.0).astype(BF16)


def dot(left, right, contract=((1,), (0,))):
    return lax.dot_general(left, right, (contract, ((), ())), preferred_element_type=F32)


def route_kernel(
    mp, per_owner, counts_from, order_from, obs_from, send_ref, base_ref, slot_ref,
    counts_ref, order_ref, obs_ref, sems,
):
    copies = [
        pltpu.make_async_copy(source, held, sems.at[index])
        for index, (source, held) in enumerate(
            ((counts_from, counts_ref), (order_from, order_ref), (obs_from, obs_ref))
        )
    ]
    for copy in copies:
        copy.start()
    copies[0].wait()
    copies[1].wait()
    blocks, capacity = order_ref.shape
    batches = counts_ref.shape[0]
    per_pair = capacity // batches
    own = lax.axis_index("group")
    ends = []
    total = jnp.int32(0)
    start = jnp.int32(0)
    for batch in range(batches):
        start = jnp.where(own == batch, total, start)
        total = total + counts_ref[batch]
        ends.append(total)
    count = counts_ref[own]
    lanes = iota((1, capacity), 1)
    batch_ids = iota((batches, capacity), 0)
    earlier = one_hot(iota((capacity, capacity), 0) < iota((capacity, capacity), 1))

    block, shift = split(start, capacity)
    first = order_ref[pl.ds(jnp.minimum(block, blocks - 1), 1), :]
    second = order_ref[pl.ds(jnp.minimum(block + 1, blocks - 1), 1), :]
    turn = lax.rem(capacity - shift, capacity)
    merged = jnp.where(lanes >= shift, first, second)
    window = pltpu.roll(jnp.broadcast_to(merged, (8, capacity)), turn, 1)[0:1]
    owner, _ = split(window, per_owner)
    filled = lanes < count
    by_owner = one_hot((batch_ids == owner) & filled)
    ahead = dot(by_owner, earlier)
    rank = jnp.sum(by_owner.astype(F32) * ahead, axis=0, keepdims=True).astype(I32)
    row_ids, rank_ids = split(iota((mp * capacity, capacity), 0), per_pair)
    row_owner, _ = split(row_ids, mp)
    target = jnp.where(filled, owner * per_pair + rank, -1)
    copies[2].wait()
    send_ref[...] = dot(
        one_hot(row_owner * per_pair + rank_ids == target), obs_ref[...]
    ).astype(send_ref.dtype)
    slot_ref[0:1, :] = jnp.where(filled, owner, -1)
    slot_ref[1:2, :] = rank

    actors = iota((per_owner, capacity), 0) + own * per_owner
    carry = jnp.zeros((batches, 1), F32)
    base = jnp.zeros((per_owner, 1), F32)
    for index in range(blocks):
        ids = order_ref[index : index + 1, :]
        here = lanes + index * capacity
        batch = jnp.zeros((1, capacity), I32)
        for end in ends:
            batch = batch + jnp.where(here >= end, 1, 0)
        mine = (ids >= own * per_owner) & (ids < (own + 1) * per_owner)
        by_batch = one_hot((batch_ids == batch) & mine)
        ahead = dot(by_batch, earlier) + carry
        wide = by_batch.astype(F32)
        place = jnp.sum(wide * ahead, axis=0, keepdims=True)
        place = place + (batch * (mp * per_pair)).astype(F32)
        carry = carry + jnp.sum(wide, axis=1, keepdims=True)
        base = base + jnp.sum(jnp.where(ids == actors, place, 0.0), axis=1, keepdims=True)
    base_ref[...] = jnp.broadcast_to(base, base_ref.shape).astype(I32)


def cell_kernel(
    mp, per_pair, offsets, base_ref, rows_ref, hidden_refs, cell_ref, input_ref, state_ref, bias_ref,
    hidden_ref, next_ref,
):
    per_owner, units = cell_ref.shape
    features = rows_ref.shape[1]
    me = lax.axis_index("mp")
    base = base_ref[:, 0:1]
    columns = iota((per_owner, rows_ref.shape[0]), 1)
    picks = jnp.concatenate([one_hot(columns == base + part * per_pair) for part in range(mp)], axis=0)
    picked = dot(picks, rows_ref[...]).astype(BF16)
    gates = None
    for part in range(mp):
        term = dot(
            picked[part * per_owner : (part + 1) * per_owner],
            input_ref[part * features : (part + 1) * features, :],
        )
        gates = term if gates is None else gates + term
    for ref, offset in zip(hidden_refs, offsets):
        rows = pl.ds(pl.multiple_of(jnp.bitwise_xor(me, offset) * units, units), units)
        gates = gates + dot(ref[...], state_ref[rows, :])
    gate = [
        gates[:, k * units : (k + 1) * units] + bias_ref[k : k + 1, :] for k in range(4)
    ]
    cell = jax.nn.sigmoid(gate[1]) * cell_ref[...].astype(F32) + jax.nn.sigmoid(gate[0]) * jnp.tanh(gate[2])
    next_ref[...] = cell.astype(BF16)
    hidden_ref[...] = (jax.nn.sigmoid(gate[3]) * jnp.tanh(cell)).astype(BF16)


def pieces(values):
    high = values.astype(BF16)
    rest = values - high.astype(F32)
    middle = rest.astype(BF16)
    low = (rest - middle.astype(F32)).astype(BF16)
    return jnp.concatenate([high, middle, low], axis=0)


def stride_of(actions):
    return -(-actions // 8) * 8


def head_kernel(
    mp, per_pair, actions, offsets, base_ref, hidden_refs, cell_ref, head_ref,
    bias_ref, value_ref, advantage_ref, send_ref, hidden_to, cell_to, sems,
):
    copies = [
        pltpu.make_async_copy(hidden_refs[0], hidden_to, sems.at[0]),
        pltpu.make_async_copy(cell_ref, cell_to, sems.at[1]),
    ]
    for copy in copies:
        copy.start()
    per_owner = base_ref.shape[0]
    units = head_ref.shape[0] // mp
    me = lax.axis_index("mp")
    total = None
    for ref, offset in zip(hidden_refs, offsets):
        rows = pl.ds(pl.multiple_of(jnp.bitwise_xor(me, offset) * units, units), units)
        term = dot(ref[...], head_ref[rows, :])
        total = term if total is None else total + term
    both = total.shape[1]
    width = both // 2
    lanes = send_ref.shape[2]
    streams = jnp.maximum(total + bias_ref[:, :both], 0.0).astype(BF16)
    first = jnp.where(me == 0, 1.0, 0.0)
    advantage = dot(streams[:, width:], advantage_ref[...], ((1,), (1,)))
    advantage = advantage + bias_ref[:, both : both + actions] * first
    value = streams[:, :width].astype(F32) * value_ref[...].astype(F32)
    value = jnp.sum(value, axis=1, keepdims=True) + bias_ref[:, both + 128 : both + 129] * first
    mixed = value + advantage - jnp.sum(advantage, axis=1, keepdims=True) * (1.0 / actions)
    lane_rank, lane_action = split(iota((actions, lanes), 1), stride_of(actions))
    to_lane = one_hot((lane_action == iota((actions, lanes), 0)) & (lane_rank < per_pair))
    spread = dot(pieces(mixed), to_lane)
    spread = spread[:per_owner] + spread[per_owner : 2 * per_owner] + spread[2 * per_owner :]
    batch, rank = split(base_ref[:, 0:1], mp * per_pair)
    lane_rank, _ = split(iota((1, lanes), 1), stride_of(actions))
    spread = jnp.where(lane_rank == rank, spread, 0.0)
    rows = send_ref.shape[0]
    to_row = one_hot(split(iota((per_owner, rows), 1), mp)[0] == batch)
    to_row = jnp.concatenate([to_row] * 3, axis=0)
    send_ref[:, 0, :] = dot(to_row, pieces(spread), ((0,), (0,)))
    for copy in copies:
        copy.wait()


def place_kernel(mp, per_pair, slot_ref, rows_ref, out_ref):
    actions, capacity = out_ref.shape
    rows, _, _ = rows_ref.shape
    stride = stride_of(actions)
    owner = slot_ref[0:1, :]
    rank = slot_ref[1:2, :]
    to_slot = one_hot(split(iota((rows, capacity), 0), mp)[0] == owner)
    to_slot = jnp.concatenate([to_slot] * 3, axis=0)
    spread = dot(pieces(rows_ref[:, 0, :]), to_slot, ((0,), (0,)))
    total = jnp.zeros((stride, capacity), F32)
    for index in range(per_pair):
        total = total + jnp.where(rank == index, spread[index * stride : (index + 1) * stride, :], 0.0)
    out_ref[...] = total[:actions, :]


def call(kernel, out_shape, specs, *args, out_specs=None, scratch=(), whole=False):
    held = [math.prod(x.shape) * x.dtype.itemsize for x in (*args, *jax.tree.leaves(out_shape))]
    return pl.pallas_call(
        kernel,
        out_shape=out_shape,
        in_specs=specs,
        out_specs=out_specs or jax.tree.map(lambda _: VMEM, out_shape),
        scratch_shapes=list(scratch),
        compiler_params=pltpu.CompilerParams(
            vmem_limit_bytes=None if whole else 2 * sum(held) + (4 << 20)
        ),
    )(*args)


def gather_parts(part, mp):
    arrays = [part]
    offsets = [0]
    distance = mp // 2
    while distance:
        pairs = [(device, device ^ distance) for device in range(mp)]
        got = []
        for array in arrays:
            got.append(lax.ppermute(array, "mp", pairs))
        arrays += got
        offsets += [offset ^ distance for offset in offsets]
        distance //= 2
    return arrays, offsets


def step(
    observations,
    hidden_state,
    cell_state,
    arrival_order,
    batch_counts,
    input_weight,
    state_weight,
    gate_bias,
    head_weight,
    head_bias,
    value_weight,
    value_bias,
    advantage_weight,
    advantage_bias,
    *,
    mp,
):
    batches = batch_counts.shape[0]
    capacity, features = observations.shape
    per_owner, units = cell_state.shape
    per_pair = capacity // batches
    actions = advantage_weight.shape[1]
    rows = batches * mp
    everyone = ("group", "mp")

    stride = stride_of(actions)
    lanes = -(-per_pair * stride // 128) * 128
    order = arrival_order.reshape(-1, capacity)

    hidden_arrays, offsets = gather_parts(hidden_state, mp)
    send, base, slot = call(
        functools.partial(route_kernel, mp, per_owner),
        (
            jax.ShapeDtypeStruct((rows * per_pair, features), BF16),
            jax.ShapeDtypeStruct((per_owner, 128), I32),
            jax.ShapeDtypeStruct((2, capacity), I32),
        ),
        [HBM, HBM, HBM],
        batch_counts,
        order,
        observations,
        scratch=(
            pltpu.SMEM(batch_counts.shape, I32),
            pltpu.VMEM(order.shape, I32),
            pltpu.VMEM(observations.shape, BF16),
            pltpu.SemaphoreType.DMA((3,)),
        ),
        whole=True,
    )
    got = lax.all_to_all(send, everyone, 0, 0, tiled=True)

    count = len(hidden_arrays)

    def cell_body(base_ref, rows_ref, *refs):
        cell_kernel(mp, per_pair, offsets, base_ref, rows_ref, refs[:count], *refs[count:])

    state = jax.ShapeDtypeStruct((per_owner, units), BF16)
    next_hidden, next_cell = call(
        cell_body,
        (state, state),
        [VMEM] * (6 + count),
        base,
        got,
        *hidden_arrays,
        cell_state,
        input_weight.reshape(input_weight.shape[0], -1),
        state_weight.reshape(state_weight.shape[0], -1),
        gate_bias,
    )

    next_arrays, _ = gather_parts(next_hidden, mp)

    def head_body(base_ref, *refs):
        head_kernel(mp, per_pair, actions, offsets, base_ref, refs[:count], *refs[count:])

    bias = jnp.concatenate(
        [head_bias.reshape(-1), jnp.pad(advantage_bias, (0, -actions % 128)), value_bias]
    )
    values, new_hidden, new_cell = call(
        head_body,
        (jax.ShapeDtypeStruct((rows, 1, lanes), F32), state, state),
        [VMEM] * (6 + count),
        base,
        *next_arrays,
        next_cell,
        head_weight.reshape(head_weight.shape[0], -1),
        bias.reshape(1, -1),
        value_weight.T,
        advantage_weight.T,
        out_specs=(VMEM, HBM, HBM),
        scratch=(pltpu.SemaphoreType.DMA((2,)),),
    )
    back = lax.all_to_all(values, everyone, 0, 0, tiled=True)
    placed = call(
        functools.partial(place_kernel, mp, per_pair),
        jax.ShapeDtypeStruct((actions, capacity), F32),
        [VMEM, VMEM],
        slot,
        back,
    )
    return placed.T, new_hidden, new_cell


def solution(mesh):
    placed = (
        P("group", "mp"),
        P("group", "mp"),
        P("group", "mp"),
        P(),
        P(),
        P(None, None, "mp"),
        P(None, None, "mp"),
        P(None, "mp"),
        P(None, None, "mp"),
        P(None, "mp"),
        P("mp", None),
        P(),
        P("mp", None),
        P(),
    )
    return jax.shard_map(
        functools.partial(step, mp=mesh.shape["mp"]),
        mesh=mesh,
        in_specs=placed,
        out_specs=(P("group", None), P("group", "mp"), P("group", "mp")),
        check_vma=False,
    )
```

```python
import functools
import math

import jax
import jax.numpy as jnp
from jax import lax
from jax.experimental import pallas as pl
from jax.experimental.pallas import tpu as pltpu
from jax.sharding import PartitionSpec as P


BF16 = jnp.bfloat16
F32 = jnp.float32
I32 = jnp.int32
VMEM = pl.BlockSpec(memory_space=pltpu.VMEM)
SMEM = pl.BlockSpec(memory_space=pltpu.SMEM)
HBM = pl.BlockSpec(memory_space=pltpu.HBM)


def iota(shape, axis):
    return lax.broadcasted_iota(I32, shape, axis)


def split(values, divisor):
    if divisor & (divisor - 1) == 0:
        quotient = lax.shift_right_logical(values, jnp.int32(divisor.bit_length() - 1))
    else:
        quotient = ((values.astype(F32) + 0.5) * (1.0 / divisor)).astype(I32)
    return quotient, values - quotient * divisor


def one_hot(mask):
    return jnp.where(mask, 1.0, 0.0).astype(BF16)


def dot(left, right, contract=((1,), (0,))):
    return lax.dot_general(left, right, (contract, ((), ())), preferred_element_type=F32)


def pieces(values):
    high = values.astype(BF16)
    rest = values - high.astype(F32)
    middle = rest.astype(BF16)
    low = (rest - middle.astype(F32)).astype(BF16)
    return jnp.concatenate([high, middle, low], axis=0)


def stride_of(actions):
    return -(-actions // 8) * 8


def span_ends(counts_ref):
    ends = []
    total = jnp.int32(0)
    for batch in range(counts_ref.shape[0]):
        total = total + counts_ref[batch]
        ends.append(total)
    return ends


def before(size):
    return one_hot(iota((size, size), 0) < iota((size, size), 1))


def route_kernel(
    mp, per_owner, counts_from, order_from, obs_from, input_from, send_to, slot_ref,
    input_ref, counts_ref, order_ref, obs_ref, send_ref, sems,
):
    copies = [
        pltpu.make_async_copy(source, held, sems.at[index])
        for index, (source, held) in enumerate(
            (
                (counts_from, counts_ref),
                (order_from, order_ref),
                (obs_from, obs_ref),
                (input_from, input_ref),
            )
        )
    ]
    for copy in copies:
        copy.start()
    blocks, capacity = order_ref.shape
    batches = counts_ref.shape[0]
    per_pair = capacity // batches
    own = lax.axis_index("group")
    lanes = iota((1, capacity), 1)
    batch_ids = iota((batches, capacity), 0)
    earlier = before(capacity)
    row_ids, rank_ids = split(iota((mp * capacity, capacity), 0), per_pair)
    row_slot = split(row_ids, mp)[0] * per_pair + rank_ids

    copies[0].wait()
    start = jnp.int32(0)
    for batch, end in enumerate(span_ends(counts_ref)):
        start = jnp.where(own == batch + 1, end, start)
    count = counts_ref[own]
    filled = lanes < count
    block, shift = split(start, capacity)
    turn = lax.rem(capacity - shift, capacity)
    copies[1].wait()
    first = order_ref[pl.ds(jnp.minimum(block, blocks - 1), 1), :]
    second = order_ref[pl.ds(jnp.minimum(block + 1, blocks - 1), 1), :]
    merged = jnp.where(lanes >= shift, first, second)
    window = pltpu.roll(jnp.broadcast_to(merged, (8, capacity)), turn, 1)[0:1]
    owner, _ = split(window, per_owner)
    by_owner = one_hot((batch_ids == owner) & filled)
    ahead = dot(by_owner, earlier)
    rank = jnp.sum(by_owner.astype(F32) * ahead, axis=0, keepdims=True).astype(I32)
    target = jnp.where(filled, owner * per_pair + rank, -1)
    copies[2].wait()
    send_ref[...] = dot(one_hot(row_slot == target), obs_ref[...]).astype(send_ref.dtype)
    out = pltpu.make_async_copy(send_ref, send_to, sems.at[4])
    out.start()
    slot_ref[0:1, :] = jnp.where(filled, owner, -1)
    slot_ref[1:2, :] = rank
    copies[3].wait()
    out.wait()


def ready_kernel(
    mp, actions, per_owner, counts_from, order_from, value_from, advantage_from, advantage_bias_from,
    hidden_from, cell_from, gate_bias_from, state_from,
    base_ref, to_row_ref, stacked_ref, stacked_bias_ref, hidden_ref, cell_ref, gate_bias_ref, state_ref,
    counts_ref, order_ref, value_ref, advantage_ref, advantage_bias_ref, sems,
):
    pairs = (
        (counts_from, counts_ref),
        (order_from, order_ref),
        (value_from, value_ref),
        (advantage_from, advantage_ref),
        (advantage_bias_from, advantage_bias_ref),
        (hidden_from, hidden_ref),
        (cell_from, cell_ref),
        (gate_bias_from, gate_bias_ref),
        (state_from, state_ref),
    )
    copies = [
        pltpu.make_async_copy(source, held, sems.at[index]) for index, (source, held) in enumerate(pairs)
    ]
    for copy in copies:
        copy.start()
    own = lax.axis_index("group")
    for copy in copies[:5]:
        copy.wait()

    blocks, capacity = order_ref.shape
    batches = counts_ref.shape[0]
    per_pair = capacity // batches
    ends = span_ends(counts_ref)
    lanes = iota((1, capacity), 1)
    batch_ids = iota((batches, capacity), 0)
    earlier = before(capacity)
    actors = iota((per_owner, capacity), 0) + own * per_owner
    carry = jnp.zeros((batches, 1), F32)
    base = jnp.zeros((per_owner, 1), F32)
    for index in range(blocks):
        ids = order_ref[index : index + 1, :]
        here = lanes + index * capacity
        batch = jnp.zeros((1, capacity), I32)
        for end in ends:
            batch = batch + jnp.where(here >= end, 1, 0)
        mine = (ids >= own * per_owner) & (ids < (own + 1) * per_owner)
        by_batch = one_hot((batch_ids == batch) & mine)
        ahead = dot(by_batch, earlier) + carry
        wide = by_batch.astype(F32)
        place = jnp.sum(wide * ahead, axis=0, keepdims=True)
        place = place + (batch * (mp * per_pair)).astype(F32)
        carry = carry + jnp.sum(wide, axis=1, keepdims=True)
        base = base + jnp.sum(jnp.where(ids == actors, place, 0.0), axis=1, keepdims=True)
    base = jnp.broadcast_to(base, base_ref.shape).astype(I32)
    base_ref[...] = base
    owner_rows = to_row_ref.shape[0]
    batch = split(jnp.concatenate([base] * 3, axis=0)[:, 0:1], mp * per_pair)[0]
    row_batch = split(iota((3 * per_owner, owner_rows), 1), mp)[0]
    to_row_ref[...] = jnp.where(row_batch == batch, 1.0, 0.0).T.astype(BF16)

    rows, both = stacked_ref.shape
    width = both // 2
    stride = stride_of(actions)
    row_rank, row_action = split(iota((rows, actions), 0), stride)
    pick = one_hot((row_action == iota((rows, actions), 1)) & (row_rank < per_pair))
    stacked_ref[:, width:] = dot(pick, advantage_ref[...]).astype(BF16)
    row_rank, row_action = split(iota((rows, width), 0), stride)
    value = jnp.broadcast_to(value_ref[...].astype(F32), (rows, width))
    stacked_ref[:, :width] = jnp.where((row_action <= actions) & (row_rank < per_pair), value, 0.0).astype(BF16)
    bias = advantage_bias_ref[...]
    bias = bias - jnp.sum(bias, axis=1, keepdims=True) * (1.0 / actions)
    spread = dot(pieces(jnp.broadcast_to(bias, (8, actions))), pick, ((1,), (1,)))
    stacked_bias_ref[...] = spread[0:1] + spread[8:9] + spread[16:17]
    for copy in copies[5:]:
        copy.wait()


def state_kernel(offsets, hidden_refs, state_ref, bias_ref, gates_ref):
    units = hidden_refs[0].shape[1]
    me = lax.axis_index("mp")
    gates = None
    for ref, offset in zip(hidden_refs, offsets):
        rows = pl.ds(pl.multiple_of(jnp.bitwise_xor(me, offset) * units, units), units)
        term = dot(ref[...], state_ref[rows, :])
        gates = term if gates is None else gates + term
    for k in range(4):
        columns = slice(k * units, (k + 1) * units)
        gates_ref[:, columns] = gates[:, columns] + bias_ref[k : k + 1, :]


def cell_kernel(mp, per_pair, base_ref, rows_ref, gates_ref, cell_ref, input_ref, hidden_ref, next_ref):
    per_owner, units = cell_ref.shape
    features = rows_ref.shape[1]
    base = base_ref[:, 0:1]
    columns = iota((per_owner, rows_ref.shape[0]), 1)
    picks = jnp.concatenate([one_hot(columns == base + part * per_pair) for part in range(mp)], axis=0)
    picked = dot(picks, rows_ref[...]).astype(BF16)
    gates = gates_ref[...]
    for part in range(mp):
        gates = gates + dot(
            picked[part * per_owner : (part + 1) * per_owner],
            input_ref[part * features : (part + 1) * features, :],
        )
    gate = [gates[:, k * units : (k + 1) * units] for k in range(4)]
    cell = jax.nn.sigmoid(gate[1]) * cell_ref[...].astype(F32) + jax.nn.sigmoid(gate[0]) * jnp.tanh(gate[2])
    next_ref[...] = cell.astype(BF16)
    hidden_ref[...] = (jax.nn.sigmoid(gate[3]) * jnp.tanh(cell)).astype(BF16)


def head_kernel(
    mp, per_pair, actions, offsets, base_ref, hidden_refs, cell_ref, head_ref, head_bias_ref,
    to_row_ref, stacked_ref, stacked_bias_ref, value_bias_ref, send_ref, hidden_to, cell_to, sems,
):
    copies = [
        pltpu.make_async_copy(hidden_refs[0], hidden_to, sems.at[0]),
        pltpu.make_async_copy(cell_ref, cell_to, sems.at[1]),
    ]
    for copy in copies:
        copy.start()
    units = head_ref.shape[0] // mp
    me = lax.axis_index("mp")
    total = None
    for ref, offset in zip(hidden_refs, offsets):
        rows = pl.ds(pl.multiple_of(jnp.bitwise_xor(me, offset) * units, units), units)
        term = dot(ref[...], head_ref[rows, :])
        total = term if total is None else total + term
    bias = jnp.concatenate([head_bias_ref[0:1, :], head_bias_ref[1:2, :]], axis=1)
    streams = jnp.maximum(total + bias, 0.0).astype(BF16)
    spread = dot(streams, stacked_ref[...], ((1,), (1,)))
    lanes = iota((1, 128), 1)
    weights = jnp.where(lanes < actions, 1.0 / actions, jnp.where(lanes == actions, -1.0, 0.0))
    mean = jnp.sum(spread[:, :128] * weights, axis=1, keepdims=True)
    spread = spread - mean + (stacked_bias_ref[...] + value_bias_ref[0]) * jnp.where(me == 0, 1.0, 0.0)
    _, rank = split(base_ref[:, 0:1], mp * per_pair)
    lane_rank, lane_action = split(iota((1, spread.shape[1]), 1), stride_of(actions))
    spread = jnp.where((lane_rank == rank) & (lane_action < actions), spread, 0.0)
    out = dot(to_row_ref[...], pieces(spread))
    chunks = out.shape[1] // 128
    for chunk in range(chunks):
        send_ref[pl.ds(chunk, out.shape[0], chunks), 0, :] = out[:, chunk * 128 : (chunk + 1) * 128]
    for copy in copies:
        copy.wait()


def place_kernel(mp, per_pair, slot_ref, rows_ref, out_ref):
    actions, capacity = out_ref.shape
    stride = stride_of(actions)
    chunks = -(-per_pair * stride // 128)
    owners = rows_ref.shape[0] // (mp * chunks)
    owner = slot_ref[0:1, :]
    rank = slot_ref[1:2, :]
    columns = []
    for chunk in range(chunks):
        total = rows_ref[pl.ds(chunk, owners, mp * chunks), 0, :]
        for part in range(1, mp):
            total = total + rows_ref[pl.ds(part * chunks + chunk, owners, mp * chunks), 0, :]
        columns.append(total)
    to_slot = one_hot(iota((owners, capacity), 0) == owner)
    to_slot = jnp.concatenate([to_slot] * 3, axis=0)
    spread = dot(pieces(jnp.concatenate(columns, axis=1)), to_slot, ((0,), (0,)))
    total = jnp.zeros((stride, capacity), F32)
    for index in range(per_pair):
        total = total + jnp.where(rank == index, spread[index * stride : (index + 1) * stride, :], 0.0)
    out_ref[...] = total[:actions, :]


def in_hbm(array):
    return pltpu.with_memory_space_constraint(array, pltpu.HBM)


def call(kernel, out_shape, specs, *args, out_specs=None, scratch=()):
    held = [math.prod(x.shape) * x.dtype.itemsize for x in (*args, *jax.tree.leaves(out_shape))]
    return pl.pallas_call(
        kernel,
        out_shape=out_shape,
        in_specs=specs,
        out_specs=out_specs or jax.tree.map(lambda _: VMEM, out_shape),
        scratch_shapes=list(scratch),
        compiler_params=pltpu.CompilerParams(vmem_limit_bytes=2 * sum(held) + (4 << 20)),
    )(*args)


def gather_parts(part, mp):
    arrays = [part]
    offsets = [0]
    distance = mp // 2
    while distance:
        pairs = [(device, device ^ distance) for device in range(mp)]
        got = []
        for array in arrays:
            got.append(lax.ppermute(array, "mp", pairs))
        arrays += got
        offsets += [offset ^ distance for offset in offsets]
        distance //= 2
    return arrays, offsets


def step(
    observations,
    hidden_state,
    cell_state,
    arrival_order,
    batch_counts,
    input_weight,
    state_weight,
    gate_bias,
    head_weight,
    head_bias,
    value_weight,
    value_bias,
    advantage_weight,
    advantage_bias,
    *,
    mp,
):
    batches = batch_counts.shape[0]
    capacity, features = observations.shape
    per_owner, units = cell_state.shape
    per_pair = capacity // batches
    actions = advantage_weight.shape[1]
    rows = batches * mp
    everyone = ("group", "mp")

    stride = stride_of(actions)
    lanes = -(-per_pair * stride // 128) * 128
    order = arrival_order.reshape(-1, capacity)

    hidden_arrays, offsets = gather_parts(hidden_state, mp)
    send, slot, input_held = call(
        functools.partial(route_kernel, mp, per_owner),
        (
            jax.ShapeDtypeStruct((rows * per_pair, features), BF16),
            jax.ShapeDtypeStruct((2, capacity), I32),
            jax.ShapeDtypeStruct(input_weight.shape, BF16),
        ),
        [HBM, HBM, HBM, HBM],
        *map(in_hbm, (batch_counts, order, observations, input_weight)),
        out_specs=(HBM, VMEM, VMEM),
        scratch=(
            pltpu.SMEM(batch_counts.shape, I32),
            pltpu.VMEM(order.shape, I32),
            pltpu.VMEM(observations.shape, BF16),
            pltpu.VMEM((rows * per_pair, features), BF16),
            pltpu.SemaphoreType.DMA((5,)),
        ),
    )
    got = lax.all_to_all(send, everyone, 0, 0, tiled=True)

    sources = (
        batch_counts,
        order,
        value_weight.T,
        advantage_weight.T,
        advantage_bias.reshape(1, -1),
        hidden_state,
        cell_state,
        gate_bias,
        state_weight,
    )
    base, to_row, stacked, stacked_bias, hidden_held, cell_held, gate_bias_held, state_held = call(
        functools.partial(ready_kernel, mp, actions, per_owner),
        (
            jax.ShapeDtypeStruct((per_owner, 128), I32),
            jax.ShapeDtypeStruct((rows, 3 * per_owner), BF16),
            jax.ShapeDtypeStruct((lanes, 2 * head_bias.shape[1]), BF16),
            jax.ShapeDtypeStruct((1, lanes), F32),
            *(jax.ShapeDtypeStruct(x.shape, x.dtype) for x in sources[5:]),
        ),
        [HBM] * len(sources),
        *map(in_hbm, sources),
        scratch=(
            pltpu.SMEM(batch_counts.shape, I32),
            *(pltpu.VMEM(x.shape, x.dtype) for x in sources[1:5]),
            pltpu.SemaphoreType.DMA((len(sources),)),
        ),
    )
    count = len(hidden_arrays)

    def state_body(*refs):
        state_kernel(offsets, refs[:count], *refs[count:])

    gates = call(
        state_body,
        jax.ShapeDtypeStruct((per_owner, 4 * units), F32),
        [VMEM] * (2 + count),
        hidden_held,
        *hidden_arrays[1:],
        state_held.reshape(state_held.shape[0], -1),
        gate_bias_held,
    )

    state = jax.ShapeDtypeStruct((per_owner, units), BF16)
    next_hidden, next_cell = call(
        functools.partial(cell_kernel, mp, per_pair),
        (state, state),
        [VMEM] * 5,
        base,
        got,
        gates,
        cell_held,
        input_held.reshape(input_held.shape[0], -1),
    )

    next_arrays = [next_hidden]
    next_offsets = [0, *(mp // 2 ^ k for k in range(mp) if k != mp // 2)]
    for offset in next_offsets[1:]:
        pairs = [(device, device ^ offset) for device in range(mp)]
        next_arrays.append(lax.ppermute(next_hidden, "mp", pairs))

    def head_body(base_ref, *refs):
        head_kernel(mp, per_pair, actions, next_offsets, base_ref, refs[:count], *refs[count:])

    values, new_hidden, new_cell = call(
        head_body,
        (jax.ShapeDtypeStruct((rows * lanes // 128, 1, 128), F32), state, state),
        [VMEM] * (7 + count) + [SMEM],
        base,
        *next_arrays,
        next_cell,
        head_weight.reshape(head_weight.shape[0], -1),
        head_bias,
        to_row,
        stacked,
        stacked_bias,
        value_bias,
        out_specs=(VMEM, HBM, HBM),
        scratch=(pltpu.SemaphoreType.DMA((2,)),),
    )
    back = lax.all_to_all(values, everyone, 0, 0, tiled=True)
    placed = call(
        functools.partial(place_kernel, mp, per_pair),
        jax.ShapeDtypeStruct((actions, capacity), F32),
        [VMEM, VMEM],
        slot,
        back,
    )
    return placed.T, new_hidden, new_cell


def solution(mesh):
    placed = (
        P("group", "mp"),
        P("group", "mp"),
        P("group", "mp"),
        P(),
        P(),
        P(None, None, "mp"),
        P(None, None, "mp"),
        P(None, "mp"),
        P(None, None, "mp"),
        P(None, "mp"),
        P("mp", None),
        P(),
        P("mp", None),
        P(),
    )
    return jax.shard_map(
        functools.partial(step, mp=mesh.shape["mp"]),
        mesh=mesh,
        in_specs=placed,
        out_specs=(P("group", None), P("group", "mp"), P("group", "mp")),
        check_vma=False,
    )
```

```python
import functools
import math

import jax
import jax.numpy as jnp
from jax import lax
from jax.experimental import pallas as pl
from jax.experimental.pallas import tpu as pltpu
from jax.sharding import PartitionSpec as P


BF16 = jnp.bfloat16
F32 = jnp.float32
I32 = jnp.int32
VMEM = pl.BlockSpec(memory_space=pltpu.VMEM)
SMEM = pl.BlockSpec(memory_space=pltpu.SMEM)
HBM = pl.BlockSpec(memory_space=pltpu.HBM)


def iota(shape, axis):
    return lax.broadcasted_iota(I32, shape, axis)


def split(values, divisor):
    if divisor & (divisor - 1) == 0:
        quotient = lax.shift_right_logical(values, jnp.int32(divisor.bit_length() - 1))
    else:
        quotient = ((values.astype(F32) + 0.5) * (1.0 / divisor)).astype(I32)
    return quotient, values - quotient * divisor


def one_hot(mask):
    return jnp.where(mask, 1.0, 0.0).astype(BF16)


def dot(left, right, contract=((1,), (0,))):
    return lax.dot_general(left, right, (contract, ((), ())), preferred_element_type=F32)


def pieces(values):
    high = values.astype(BF16)
    rest = values - high.astype(F32)
    middle = rest.astype(BF16)
    low = (rest - middle.astype(F32)).astype(BF16)
    return jnp.concatenate([high, middle, low], axis=0)


def stride_of(actions):
    return -(-(actions + 1) // 8) * 8


def span_ends(counts_ref):
    ends = []
    total = jnp.int32(0)
    for batch in range(counts_ref.shape[0]):
        total = total + counts_ref[batch]
        ends.append(total)
    return ends


def before(size):
    return one_hot(iota((size, size), 0) < iota((size, size), 1))


def route_kernel(
    mp, per_owner, counts_from, order_from, obs_from, state_from, send_to, slot_ref,
    state_ref, counts_ref, order_ref, obs_ref, send_ref, sems,
):
    copies = [
        pltpu.make_async_copy(source, held, sems.at[index])
        for index, (source, held) in enumerate(
            (
                (counts_from, counts_ref),
                (order_from, order_ref),
                (obs_from, obs_ref),
                (state_from, state_ref),
            )
        )
    ]
    for copy in copies:
        copy.start()
    blocks, capacity = order_ref.shape
    batches = counts_ref.shape[0]
    per_pair = capacity // batches
    own = lax.axis_index("group")
    lanes = iota((1, capacity), 1)
    batch_ids = iota((batches, capacity), 0)
    earlier = before(capacity)
    row_ids, rank_ids = split(iota((mp * capacity, capacity), 0), per_pair)
    row_slot = split(row_ids, mp)[0] * per_pair + rank_ids

    copies[0].wait()
    start = jnp.int32(0)
    for batch, end in enumerate(span_ends(counts_ref)):
        start = jnp.where(own == batch + 1, end, start)
    count = counts_ref[own]
    filled = lanes < count
    block, shift = split(start, capacity)
    turn = lax.rem(capacity - shift, capacity)
    copies[1].wait()
    first = order_ref[pl.ds(jnp.minimum(block, blocks - 1), 1), :]
    second = order_ref[pl.ds(jnp.minimum(block + 1, blocks - 1), 1), :]
    merged = jnp.where(lanes >= shift, first, second)
    window = pltpu.roll(jnp.broadcast_to(merged, (8, capacity)), turn, 1)[0:1]
    owner, _ = split(window, per_owner)
    by_owner = one_hot((batch_ids == owner) & filled)
    ahead = dot(by_owner, earlier)
    rank = jnp.sum(by_owner.astype(F32) * ahead, axis=0, keepdims=True).astype(I32)
    target = jnp.where(filled, owner * per_pair + rank, -1)
    copies[2].wait()
    send_ref[...] = dot(one_hot(row_slot == target), obs_ref[...]).astype(send_ref.dtype)
    out = pltpu.make_async_copy(send_ref, send_to, sems.at[4])
    out.start()
    slot_ref[0:1, :] = jnp.where(filled, owner, -1)
    slot_ref[1:2, :] = rank
    copies[3].wait()
    out.wait()


def ready_kernel(
    mp, actions, per_owner, counts_from, order_from, value_from, advantage_from, advantage_bias_from,
    hidden_from, cell_from, gate_bias_from, input_from,
    base_ref, picks_ref, to_row_ref, stacked_ref, stacked_bias_ref, hidden_ref, cell_ref, gate_bias_ref, input_ref,
    counts_ref, order_ref, value_ref, advantage_ref, advantage_bias_ref, sems,
):
    pairs = (
        (counts_from, counts_ref),
        (order_from, order_ref),
        (value_from, value_ref),
        (advantage_from, advantage_ref),
        (advantage_bias_from, advantage_bias_ref),
        (hidden_from, hidden_ref),
        (cell_from, cell_ref),
        (gate_bias_from, gate_bias_ref),
        (input_from, input_ref),
    )
    copies = [
        pltpu.make_async_copy(source, held, sems.at[index]) for index, (source, held) in enumerate(pairs)
    ]
    for copy in copies:
        copy.start()
    own = lax.axis_index("group")
    for copy in copies[:5]:
        copy.wait()

    blocks, capacity = order_ref.shape
    batches = counts_ref.shape[0]
    per_pair = capacity // batches
    ends = span_ends(counts_ref)
    lanes = iota((1, capacity), 1)
    batch_ids = iota((batches, capacity), 0)
    earlier = before(capacity)
    actors = iota((per_owner, capacity), 0) + own * per_owner
    carry = jnp.zeros((batches, 1), F32)
    base = jnp.zeros((per_owner, 1), F32)
    for index in range(blocks):
        ids = order_ref[index : index + 1, :]
        here = lanes + index * capacity
        batch = jnp.zeros((1, capacity), I32)
        for end in ends:
            batch = batch + jnp.where(here >= end, 1, 0)
        mine = (ids >= own * per_owner) & (ids < (own + 1) * per_owner)
        by_batch = one_hot((batch_ids == batch) & mine)
        ahead = dot(by_batch, earlier) + carry
        wide = by_batch.astype(F32)
        place = jnp.sum(wide * ahead, axis=0, keepdims=True)
        place = place + (batch * (mp * per_pair)).astype(F32)
        carry = carry + jnp.sum(wide, axis=1, keepdims=True)
        base = base + jnp.sum(jnp.where(ids == actors, place, 0.0), axis=1, keepdims=True)
    base = jnp.broadcast_to(base, base_ref.shape).astype(I32)
    base_ref[...] = base
    columns = iota((per_owner, picks_ref.shape[1]), 1)
    for part in range(mp):
        mask = columns == base[:, 0:1] + part * per_pair
        picks_ref[part * per_owner : (part + 1) * per_owner, :] = one_hot(mask)
    owner_rows = to_row_ref.shape[0]
    batch = split(jnp.concatenate([base] * 3, axis=0)[:, 0:1], mp * per_pair)[0]
    row_batch = split(iota((3 * per_owner, owner_rows), 1), mp)[0]
    to_row_ref[...] = jnp.where(row_batch == batch, 1.0, 0.0).T.astype(BF16)

    rows, both = stacked_ref.shape
    width = both // 2
    stride = stride_of(actions)
    row_rank, row_action = split(iota((rows, actions), 0), stride)
    pick = one_hot((row_action == iota((rows, actions), 1)) & (row_rank < per_pair))
    stacked_ref[:, width:] = dot(pick, advantage_ref[...]).astype(BF16)
    row_rank, row_action = split(iota((rows, width), 0), stride)
    value = jnp.broadcast_to(value_ref[...].astype(F32), (rows, width))
    stacked_ref[:, :width] = jnp.where((row_action <= actions) & (row_rank < per_pair), value, 0.0).astype(BF16)
    bias = advantage_bias_ref[...]
    spread = dot(pieces(jnp.broadcast_to(bias, (8, actions))), pick, ((1,), (1,)))
    stacked_bias_ref[...] = spread[0:1] + spread[8:9] + spread[16:17]
    for copy in copies[5:]:
        copy.wait()


def state_kernel(offsets, hidden_refs, state_ref, bias_ref, gates_ref):
    units = hidden_refs[0].shape[1]
    me = lax.axis_index("mp")
    gates = None
    for ref, offset in zip(hidden_refs, offsets):
        rows = pl.ds(pl.multiple_of(jnp.bitwise_xor(me, offset) * units, units), units)
        term = dot(ref[...], state_ref[rows, :])
        gates = term if gates is None else gates + term
    for k in range(4):
        columns = slice(k * units, (k + 1) * units)
        gates_ref[:, columns] = gates[:, columns] + bias_ref[k : k + 1, :]


def cell_kernel(mp, picks_ref, rows_ref, gates_ref, cell_ref, input_ref, hidden_ref, next_ref):
    per_owner, units = cell_ref.shape
    features = rows_ref.shape[1]
    picked = dot(picks_ref[...], rows_ref[...]).astype(BF16)
    gates = gates_ref[...]
    for part in range(mp):
        gates = gates + dot(
            picked[part * per_owner : (part + 1) * per_owner],
            input_ref[part * features : (part + 1) * features, :],
        )
    gate = [gates[:, k * units : (k + 1) * units] for k in range(4)]
    cell = jax.nn.sigmoid(gate[1]) * cell_ref[...].astype(F32) + jax.nn.sigmoid(gate[0]) * jnp.tanh(gate[2])
    next_ref[...] = cell.astype(BF16)
    hidden_ref[...] = (jax.nn.sigmoid(gate[3]) * jnp.tanh(cell)).astype(BF16)


def head_kernel(
    mp, per_pair, actions, offsets, base_ref, hidden_refs, cell_ref, head_ref, head_bias_ref,
    to_row_ref, stacked_ref, stacked_bias_ref, value_bias_ref, send_ref, hidden_to, cell_to, sems,
):
    copies = [
        pltpu.make_async_copy(hidden_refs[0], hidden_to, sems.at[0]),
        pltpu.make_async_copy(cell_ref, cell_to, sems.at[1]),
    ]
    for copy in copies:
        copy.start()
    units = head_ref.shape[0] // mp
    me = lax.axis_index("mp")
    total = None
    for ref, offset in zip(hidden_refs, offsets):
        rows = pl.ds(pl.multiple_of(jnp.bitwise_xor(me, offset) * units, units), units)
        term = dot(ref[...], head_ref[rows, :])
        total = term if total is None else total + term
    bias = jnp.concatenate([head_bias_ref[0:1, :], head_bias_ref[1:2, :]], axis=1)
    streams = jnp.maximum(total + bias, 0.0).astype(BF16)
    spread = dot(streams, stacked_ref[...], ((1,), (1,)))
    spread = spread + (stacked_bias_ref[...] + value_bias_ref[0]) * jnp.where(me == 0, 1.0, 0.0)
    _, rank = split(base_ref[:, 0:1], mp * per_pair)
    lane_rank, _ = split(iota((1, spread.shape[1]), 1), stride_of(actions))
    spread = jnp.where(lane_rank == rank, spread, 0.0)
    out = dot(to_row_ref[...], pieces(spread))
    chunks = out.shape[1] // 128
    for chunk in range(chunks):
        send_ref[pl.ds(chunk, out.shape[0], chunks), 0, :] = out[:, chunk * 128 : (chunk + 1) * 128]
    for copy in copies:
        copy.wait()


def place_kernel(mp, per_pair, slot_ref, rows_ref, out_ref):
    actions, capacity = out_ref.shape
    stride = stride_of(actions)
    chunks = -(-per_pair * stride // 128)
    owners = rows_ref.shape[0] // (mp * chunks)
    owner = slot_ref[0:1, :]
    rank = slot_ref[1:2, :]
    columns = []
    for chunk in range(chunks):
        total = rows_ref[pl.ds(chunk, owners, mp * chunks), 0, :]
        for part in range(1, mp):
            total = total + rows_ref[pl.ds(part * chunks + chunk, owners, mp * chunks), 0, :]
        columns.append(total)
    to_slot = one_hot(iota((owners, capacity), 0) == owner)
    to_slot = jnp.concatenate([to_slot] * 3, axis=0)
    spread = dot(pieces(jnp.concatenate(columns, axis=1)), to_slot, ((0,), (0,)))
    total = jnp.zeros((stride, capacity), F32)
    for index in range(per_pair):
        total = total + jnp.where(rank == index, spread[index * stride : (index + 1) * stride, :], 0.0)
    row = iota((stride, capacity), 0)
    weights = jnp.where(row < actions, 1.0 / actions, jnp.where(row == actions, -1.0, 0.0))
    total = total - jnp.sum(total * weights, axis=0, keepdims=True)
    out_ref[...] = total[:actions, :]


def in_hbm(array):
    return pltpu.with_memory_space_constraint(array, pltpu.HBM)


def call(kernel, out_shape, specs, *args, out_specs=None, scratch=()):
    held = [math.prod(x.shape) * x.dtype.itemsize for x in (*args, *jax.tree.leaves(out_shape))]
    return pl.pallas_call(
        kernel,
        out_shape=out_shape,
        in_specs=specs,
        out_specs=out_specs or jax.tree.map(lambda _: VMEM, out_shape),
        scratch_shapes=list(scratch),
        compiler_params=pltpu.CompilerParams(vmem_limit_bytes=2 * sum(held) + (4 << 20)),
    )(*args)


def gather_parts(part, mp):
    arrays = [part]
    offsets = [0]
    distance = mp // 2
    while distance:
        pairs = [(device, device ^ distance) for device in range(mp)]
        got = []
        for array in arrays:
            got.append(lax.ppermute(array, "mp", pairs))
        arrays += got
        offsets += [offset ^ distance for offset in offsets]
        distance //= 2
    return arrays, offsets


def step(
    observations,
    hidden_state,
    cell_state,
    arrival_order,
    batch_counts,
    input_weight,
    state_weight,
    gate_bias,
    head_weight,
    head_bias,
    value_weight,
    value_bias,
    advantage_weight,
    advantage_bias,
    *,
    mp,
):
    batches = batch_counts.shape[0]
    capacity, features = observations.shape
    per_owner, units = cell_state.shape
    per_pair = capacity // batches
    actions = advantage_weight.shape[1]
    rows = batches * mp
    everyone = ("group", "mp")

    stride = stride_of(actions)
    lanes = -(-per_pair * stride // 128) * 128
    order = arrival_order.reshape(-1, capacity)

    hidden_arrays, offsets = gather_parts(hidden_state, mp)
    send, slot, state_held = call(
        functools.partial(route_kernel, mp, per_owner),
        (
            jax.ShapeDtypeStruct((rows * per_pair, features), BF16),
            jax.ShapeDtypeStruct((2, capacity), I32),
            jax.ShapeDtypeStruct(state_weight.shape, BF16),
        ),
        [HBM, HBM, HBM, HBM],
        *map(in_hbm, (batch_counts, order, observations, state_weight)),
        out_specs=(HBM, VMEM, VMEM),
        scratch=(
            pltpu.SMEM(batch_counts.shape, I32),
            pltpu.VMEM(order.shape, I32),
            pltpu.VMEM(observations.shape, BF16),
            pltpu.VMEM((rows * per_pair, features), BF16),
            pltpu.SemaphoreType.DMA((5,)),
        ),
    )
    got = lax.all_to_all(send, everyone, 0, 0, tiled=True)

    sources = (
        batch_counts,
        order,
        value_weight.T,
        advantage_weight.T,
        advantage_bias.reshape(1, -1),
        hidden_state,
        cell_state,
        gate_bias,
        input_weight,
    )
    base, picks, to_row, stacked, stacked_bias, hidden_held, cell_held, gate_bias_held, input_held = call(
        functools.partial(ready_kernel, mp, actions, per_owner),
        (
            jax.ShapeDtypeStruct((per_owner, 128), I32),
            jax.ShapeDtypeStruct((mp * per_owner, rows * per_pair), BF16),
            jax.ShapeDtypeStruct((rows, 3 * per_owner), BF16),
            jax.ShapeDtypeStruct((lanes, 2 * head_bias.shape[1]), BF16),
            jax.ShapeDtypeStruct((1, lanes), F32),
            *(jax.ShapeDtypeStruct(x.shape, x.dtype) for x in sources[5:]),
        ),
        [HBM] * len(sources),
        *map(in_hbm, sources),
        scratch=(
            pltpu.SMEM(batch_counts.shape, I32),
            *(pltpu.VMEM(x.shape, x.dtype) for x in sources[1:5]),
            pltpu.SemaphoreType.DMA((len(sources),)),
        ),
    )
    count = len(hidden_arrays)

    def state_body(*refs):
        state_kernel(offsets, refs[:count], *refs[count:])

    gates = call(
        state_body,
        jax.ShapeDtypeStruct((per_owner, 4 * units), F32),
        [VMEM] * (2 + count),
        hidden_held,
        *hidden_arrays[1:],
        state_held.reshape(state_held.shape[0], -1),
        gate_bias_held,
    )

    state = jax.ShapeDtypeStruct((per_owner, units), BF16)
    next_hidden, next_cell = call(
        functools.partial(cell_kernel, mp),
        (state, state),
        [VMEM] * 5,
        picks,
        got,
        gates,
        cell_held,
        input_held.reshape(input_held.shape[0], -1),
    )

    next_arrays = [next_hidden]
    next_offsets = [0, *(mp // 2 ^ k for k in range(mp) if k != mp // 2)]
    for offset in next_offsets[1:]:
        pairs = [(device, device ^ offset) for device in range(mp)]
        next_arrays.append(lax.ppermute(next_hidden, "mp", pairs))

    def head_body(base_ref, *refs):
        head_kernel(mp, per_pair, actions, next_offsets, base_ref, refs[:count], *refs[count:])

    values, new_hidden, new_cell = call(
        head_body,
        (jax.ShapeDtypeStruct((rows * lanes // 128, 1, 128), F32), state, state),
        [VMEM] * (7 + count) + [SMEM],
        base,
        *next_arrays,
        next_cell,
        head_weight.reshape(head_weight.shape[0], -1),
        head_bias,
        to_row,
        stacked,
        stacked_bias,
        value_bias,
        out_specs=(VMEM, HBM, HBM),
        scratch=(pltpu.SemaphoreType.DMA((2,)),),
    )
    back = lax.all_to_all(values, everyone, 0, 0, tiled=True)
    placed = call(
        functools.partial(place_kernel, mp, per_pair),
        jax.ShapeDtypeStruct((actions, capacity), F32),
        [VMEM, VMEM],
        slot,
        back,
    )
    return placed.T, new_hidden, new_cell


def solution(mesh):
    placed = (
        P("group", "mp"),
        P("group", "mp"),
        P("group", "mp"),
        P(),
        P(),
        P(None, None, "mp"),
        P(None, None, "mp"),
        P(None, "mp"),
        P(None, None, "mp"),
        P(None, "mp"),
        P("mp", None),
        P(),
        P("mp", None),
        P(),
    )
    return jax.shard_map(
        functools.partial(step, mp=mesh.shape["mp"]),
        mesh=mesh,
        in_specs=placed,
        out_specs=(P("group", None), P("group", "mp"), P("group", "mp")),
        check_vma=False,
    )
```

```python
import functools
import math

import jax
import jax.numpy as jnp
from jax import lax
from jax.experimental import pallas as pl
from jax.experimental.pallas import tpu as pltpu
from jax.sharding import PartitionSpec as P


BF16 = jnp.bfloat16
F32 = jnp.float32
I32 = jnp.int32
VMEM = pl.BlockSpec(memory_space=pltpu.VMEM)
SMEM = pl.BlockSpec(memory_space=pltpu.SMEM)
HBM = pl.BlockSpec(memory_space=pltpu.HBM)


def iota(shape, axis):
    return lax.broadcasted_iota(I32, shape, axis)


def split(values, divisor):
    if divisor & (divisor - 1) == 0:
        quotient = lax.shift_right_logical(values, jnp.int32(divisor.bit_length() - 1))
    else:
        quotient = ((values.astype(F32) + 0.5) * (1.0 / divisor)).astype(I32)
    return quotient, values - quotient * divisor


def one_hot(mask):
    return jnp.where(mask, 1.0, 0.0).astype(BF16)


def dot(left, right, contract=((1,), (0,))):
    return lax.dot_general(left, right, (contract, ((), ())), preferred_element_type=F32)


def pieces(values):
    high = values.astype(BF16)
    rest = values - high.astype(F32)
    middle = rest.astype(BF16)
    low = (rest - middle.astype(F32)).astype(BF16)
    return jnp.concatenate([high, middle, low], axis=0)


def stride_of(actions):
    return -(-(actions + 1) // 8) * 8


def span_ends(counts_ref):
    ends = []
    total = jnp.int32(0)
    for batch in range(counts_ref.shape[0]):
        total = total + counts_ref[batch]
        ends.append(total)
    return ends


def before(size):
    return one_hot(iota((size, size), 0) < iota((size, size), 1))


def route_kernel(
    mp, per_owner, counts_from, order_from, obs_from, state_from, send_to, slot_ref,
    state_ref, counts_ref, order_ref, obs_ref, send_ref, sems,
):
    copies = [
        pltpu.make_async_copy(source, held, sems.at[index])
        for index, (source, held) in enumerate(
            (
                (counts_from, counts_ref),
                (order_from, order_ref),
                (obs_from, obs_ref),
                (state_from, state_ref),
            )
        )
    ]
    for copy in copies:
        copy.start()
    blocks, capacity = order_ref.shape
    batches = counts_ref.shape[0]
    per_pair = capacity // batches
    own = lax.axis_index("group")
    lanes = iota((1, capacity), 1)
    batch_ids = iota((batches, capacity), 0)
    earlier = before(capacity)
    row_ids, rank_ids = split(iota((mp * capacity, capacity), 0), per_pair)
    row_slot = split(row_ids, mp)[0] * per_pair + rank_ids

    copies[0].wait()
    start = jnp.int32(0)
    for batch, end in enumerate(span_ends(counts_ref)):
        start = jnp.where(own == batch + 1, end, start)
    count = counts_ref[own]
    filled = lanes < count
    block, shift = split(start, capacity)
    turn = lax.rem(capacity - shift, capacity)
    copies[1].wait()
    first = order_ref[pl.ds(jnp.minimum(block, blocks - 1), 1), :]
    second = order_ref[pl.ds(jnp.minimum(block + 1, blocks - 1), 1), :]
    merged = jnp.where(lanes >= shift, first, second)
    window = pltpu.roll(jnp.broadcast_to(merged, (8, capacity)), turn, 1)[0:1]
    owner, _ = split(window, per_owner)
    by_owner = one_hot((batch_ids == owner) & filled)
    ahead = dot(by_owner, earlier)
    rank = jnp.sum(by_owner.astype(F32) * ahead, axis=0, keepdims=True).astype(I32)
    target = jnp.where(filled, owner * per_pair + rank, -1)
    copies[2].wait()
    send_ref[...] = dot(one_hot(row_slot == target), obs_ref[...]).astype(send_ref.dtype)
    out = pltpu.make_async_copy(send_ref, send_to, sems.at[4])
    out.start()
    slot_ref[0:1, :] = jnp.where(filled, owner, -1)
    slot_ref[1:2, :] = rank
    copies[3].wait()
    out.wait()


def ready_kernel(
    mp, actions, per_owner, counts_from, order_from, value_from, advantage_from, advantage_bias_from,
    hidden_from, cell_from, gate_bias_from, input_from,
    base_ref, picks_ref, to_row_ref, stacked_ref, stacked_bias_ref, hidden_ref, cell_ref, gate_bias_ref, input_ref,
    counts_ref, order_ref, value_ref, advantage_ref, advantage_bias_ref, sems,
):
    pairs = (
        (counts_from, counts_ref),
        (order_from, order_ref),
        (value_from, value_ref),
        (advantage_from, advantage_ref),
        (advantage_bias_from, advantage_bias_ref),
        (hidden_from, hidden_ref),
        (cell_from, cell_ref),
        (gate_bias_from, gate_bias_ref),
        (input_from, input_ref),
    )
    copies = [
        pltpu.make_async_copy(source, held, sems.at[index]) for index, (source, held) in enumerate(pairs)
    ]
    for copy in copies:
        copy.start()
    own = lax.axis_index("group")
    for copy in copies[:5]:
        copy.wait()

    blocks, capacity = order_ref.shape
    batches = counts_ref.shape[0]
    per_pair = capacity // batches
    ends = span_ends(counts_ref)
    lanes = iota((1, capacity), 1)
    batch_ids = iota((batches, capacity), 0)
    earlier = before(capacity)
    actors = iota((per_owner, capacity), 0) + own * per_owner
    carry = jnp.zeros((batches, 1), F32)
    base = jnp.zeros((per_owner, 1), F32)
    for index in range(blocks):
        ids = order_ref[index : index + 1, :]
        here = lanes + index * capacity
        batch = jnp.zeros((1, capacity), I32)
        for end in ends:
            batch = batch + jnp.where(here >= end, 1, 0)
        mine = (ids >= own * per_owner) & (ids < (own + 1) * per_owner)
        by_batch = one_hot((batch_ids == batch) & mine)
        ahead = dot(by_batch, earlier) + carry
        wide = by_batch.astype(F32)
        place = jnp.sum(wide * ahead, axis=0, keepdims=True)
        place = place + (batch * (mp * per_pair)).astype(F32)
        carry = carry + jnp.sum(wide, axis=1, keepdims=True)
        base = base + jnp.sum(jnp.where(ids == actors, place, 0.0), axis=1, keepdims=True)
    base = jnp.broadcast_to(base, base_ref.shape).astype(I32)
    base_ref[...] = base
    columns = iota((per_owner, picks_ref.shape[1]), 1)
    for part in range(mp):
        mask = columns == base[:, 0:1] + part * per_pair
        picks_ref[part * per_owner : (part + 1) * per_owner, :] = one_hot(mask)
    owner_rows = to_row_ref.shape[0]
    batch = split(jnp.concatenate([base] * 3, axis=0)[:, 0:1], mp * per_pair)[0]
    row_batch = split(iota((3 * per_owner, owner_rows), 1), mp)[0]
    to_row_ref[...] = jnp.where(row_batch == batch, 1.0, 0.0).T.astype(BF16)

    rows, both = stacked_ref.shape
    width = both // 2
    stride = stride_of(actions)
    row_rank, row_action = split(iota((rows, actions), 0), stride)
    pick = one_hot((row_action == iota((rows, actions), 1)) & (row_rank < per_pair))
    stacked_ref[:, width:] = dot(pick, advantage_ref[...]).astype(BF16)
    row_rank, row_action = split(iota((rows, width), 0), stride)
    value = jnp.broadcast_to(value_ref[...].astype(F32), (rows, width))
    stacked_ref[:, :width] = jnp.where((row_action <= actions) & (row_rank < per_pair), value, 0.0).astype(BF16)
    bias = advantage_bias_ref[...]
    spread = dot(pieces(jnp.broadcast_to(bias, (8, actions))), pick, ((1,), (1,)))
    stacked_bias_ref[...] = spread[0:1] + spread[8:9] + spread[16:17]
    for copy in copies[5:]:
        copy.wait()


def state_kernel(offsets, hidden_refs, state_ref, bias_ref, gates_ref):
    units = hidden_refs[0].shape[1]
    me = lax.axis_index("mp")
    gates = None
    for ref, offset in zip(hidden_refs, offsets):
        rows = pl.ds(pl.multiple_of(jnp.bitwise_xor(me, offset) * units, units), units)
        term = dot(ref[...], state_ref[rows, :])
        gates = term if gates is None else gates + term
    for k in range(4):
        columns = slice(k * units, (k + 1) * units)
        gates_ref[:, columns] = gates[:, columns] + bias_ref[k : k + 1, :]


def cell_kernel(mp, picks_ref, rows_ref, gates_ref, cell_ref, input_ref, hidden_ref, next_ref):
    per_owner, units = cell_ref.shape
    features = rows_ref.shape[1]
    picked = dot(picks_ref[...], rows_ref[...]).astype(BF16)
    gates = gates_ref[...]
    for part in range(mp):
        gates = gates + dot(
            picked[part * per_owner : (part + 1) * per_owner],
            input_ref[part * features : (part + 1) * features, :],
        )
    gate = [gates[:, k * units : (k + 1) * units] for k in range(4)]
    cell = jax.nn.sigmoid(gate[1]) * cell_ref[...].astype(F32) + jax.nn.sigmoid(gate[0]) * jnp.tanh(gate[2])
    next_ref[...] = cell.astype(BF16)
    hidden_ref[...] = (jax.nn.sigmoid(gate[3]) * jnp.tanh(cell)).astype(BF16)


def head_products(offsets, hidden_refs, head_ref):
    units = hidden_refs[0].shape[1]
    me = lax.axis_index("mp")
    total = None
    for ref, offset in zip(hidden_refs, offsets):
        rows = pl.ds(pl.multiple_of(jnp.bitwise_xor(me, offset) * units, units), units)
        term = dot(ref[...], head_ref[rows, :])
        total = term if total is None else total + term
    return total


def early_kernel(offsets, hidden_refs, cell_ref, head_ref, head_bias_ref, total_ref, hidden_to, cell_to, sems):
    copies = [
        pltpu.make_async_copy(hidden_refs[0], hidden_to, sems.at[0]),
        pltpu.make_async_copy(cell_ref, cell_to, sems.at[1]),
    ]
    for copy in copies:
        copy.start()
    bias = jnp.concatenate([head_bias_ref[0:1, :], head_bias_ref[1:2, :]], axis=1)
    total_ref[...] = head_products(offsets, hidden_refs, head_ref) + bias
    for copy in copies:
        copy.wait()


def middle_kernel(offsets, hidden_refs, head_ref, from_ref, total_ref):
    total_ref[...] = from_ref[...] + head_products(offsets, hidden_refs, head_ref)


def head_kernel(
    mp, per_pair, actions, offsets, base_ref, total_ref, hidden_refs, head_ref, to_row_ref, stacked_ref,
    stacked_bias_ref, value_bias_ref, send_ref,
):
    total = total_ref[...] + head_products(offsets, hidden_refs, head_ref)
    streams = jnp.maximum(total, 0.0).astype(BF16)
    spread = dot(streams, stacked_ref[...], ((1,), (1,)))
    first = jnp.where(lax.axis_index("mp") == 0, 1.0, 0.0)
    spread = spread + (stacked_bias_ref[...] + value_bias_ref[0]) * first
    _, rank = split(base_ref[:, 0:1], mp * per_pair)
    lane_rank, _ = split(iota((1, spread.shape[1]), 1), stride_of(actions))
    spread = jnp.where(lane_rank == rank, spread, 0.0)
    out = dot(to_row_ref[...], pieces(spread))
    chunks = out.shape[1] // 128
    for chunk in range(chunks):
        send_ref[pl.ds(chunk, out.shape[0], chunks), 0, :] = out[:, chunk * 128 : (chunk + 1) * 128]


def place_kernel(mp, per_pair, slot_ref, rows_ref, out_ref):
    actions, capacity = out_ref.shape
    stride = stride_of(actions)
    chunks = -(-per_pair * stride // 128)
    owners = rows_ref.shape[0] // (mp * chunks)
    owner = slot_ref[0:1, :]
    rank = slot_ref[1:2, :]
    columns = []
    for chunk in range(chunks):
        total = rows_ref[pl.ds(chunk, owners, mp * chunks), 0, :]
        for part in range(1, mp):
            total = total + rows_ref[pl.ds(part * chunks + chunk, owners, mp * chunks), 0, :]
        columns.append(total)
    to_slot = one_hot(iota((owners, capacity), 0) == owner)
    to_slot = jnp.concatenate([to_slot] * 3, axis=0)
    spread = dot(pieces(jnp.concatenate(columns, axis=1)), to_slot, ((0,), (0,)))
    total = jnp.zeros((stride, capacity), F32)
    for index in range(per_pair):
        total = total + jnp.where(rank == index, spread[index * stride : (index + 1) * stride, :], 0.0)
    row = iota((stride, capacity), 0)
    weights = jnp.where(row < actions, 1.0 / actions, jnp.where(row == actions, -1.0, 0.0))
    total = total - jnp.sum(total * weights, axis=0, keepdims=True)
    out_ref[...] = total[:actions, :]


def in_hbm(array):
    return pltpu.with_memory_space_constraint(array, pltpu.HBM)


def call(kernel, out_shape, specs, *args, out_specs=None, scratch=()):
    held = [math.prod(x.shape) * x.dtype.itemsize for x in (*args, *jax.tree.leaves(out_shape))]
    return pl.pallas_call(
        kernel,
        out_shape=out_shape,
        in_specs=specs,
        out_specs=out_specs or jax.tree.map(lambda _: VMEM, out_shape),
        scratch_shapes=list(scratch),
        compiler_params=pltpu.CompilerParams(vmem_limit_bytes=2 * sum(held) + (4 << 20)),
    )(*args)


def gather_parts(part, mp):
    arrays = [part]
    offsets = [0]
    distance = mp // 2
    while distance:
        pairs = [(device, device ^ distance) for device in range(mp)]
        got = []
        for array in arrays:
            got.append(lax.ppermute(array, "mp", pairs))
        arrays += got
        offsets += [offset ^ distance for offset in offsets]
        distance //= 2
    return arrays, offsets


def step(
    observations,
    hidden_state,
    cell_state,
    arrival_order,
    batch_counts,
    input_weight,
    state_weight,
    gate_bias,
    head_weight,
    head_bias,
    value_weight,
    value_bias,
    advantage_weight,
    advantage_bias,
    *,
    mp,
):
    batches = batch_counts.shape[0]
    capacity, features = observations.shape
    per_owner, units = cell_state.shape
    per_pair = capacity // batches
    actions = advantage_weight.shape[1]
    rows = batches * mp
    everyone = ("group", "mp")

    stride = stride_of(actions)
    lanes = -(-per_pair * stride // 128) * 128
    order = arrival_order.reshape(-1, capacity)

    hidden_arrays, offsets = gather_parts(hidden_state, mp)
    send, slot, state_held = call(
        functools.partial(route_kernel, mp, per_owner),
        (
            jax.ShapeDtypeStruct((rows * per_pair, features), BF16),
            jax.ShapeDtypeStruct((2, capacity), I32),
            jax.ShapeDtypeStruct(state_weight.shape, BF16),
        ),
        [HBM, HBM, HBM, HBM],
        *map(in_hbm, (batch_counts, order, observations, state_weight)),
        out_specs=(HBM, VMEM, VMEM),
        scratch=(
            pltpu.SMEM(batch_counts.shape, I32),
            pltpu.VMEM(order.shape, I32),
            pltpu.VMEM(observations.shape, BF16),
            pltpu.VMEM((rows * per_pair, features), BF16),
            pltpu.SemaphoreType.DMA((5,)),
        ),
    )
    got = lax.all_to_all(send, everyone, 0, 0, tiled=True)

    sources = (
        batch_counts,
        order,
        value_weight.T,
        advantage_weight.T,
        advantage_bias.reshape(1, -1),
        hidden_state,
        cell_state,
        gate_bias,
        input_weight,
    )
    base, picks, to_row, stacked, stacked_bias, hidden_held, cell_held, gate_bias_held, input_held = call(
        functools.partial(ready_kernel, mp, actions, per_owner),
        (
            jax.ShapeDtypeStruct((per_owner, 128), I32),
            jax.ShapeDtypeStruct((mp * per_owner, rows * per_pair), BF16),
            jax.ShapeDtypeStruct((rows, 3 * per_owner), BF16),
            jax.ShapeDtypeStruct((lanes, 2 * head_bias.shape[1]), BF16),
            jax.ShapeDtypeStruct((1, lanes), F32),
            *(jax.ShapeDtypeStruct(x.shape, x.dtype) for x in sources[5:]),
        ),
        [HBM] * len(sources),
        *map(in_hbm, sources),
        scratch=(
            pltpu.SMEM(batch_counts.shape, I32),
            *(pltpu.VMEM(x.shape, x.dtype) for x in sources[1:5]),
            pltpu.SemaphoreType.DMA((len(sources),)),
        ),
    )
    count = len(hidden_arrays)

    def state_body(*refs):
        state_kernel(offsets, refs[:count], *refs[count:])

    gates = call(
        state_body,
        jax.ShapeDtypeStruct((per_owner, 4 * units), F32),
        [VMEM] * (2 + count),
        hidden_held,
        *hidden_arrays[1:],
        state_held.reshape(state_held.shape[0], -1),
        gate_bias_held,
    )

    state = jax.ShapeDtypeStruct((per_owner, units), BF16)
    next_hidden, next_cell = call(
        functools.partial(cell_kernel, mp),
        (state, state),
        [VMEM] * 5,
        picks,
        got,
        gates,
        cell_held,
        input_held.reshape(input_held.shape[0], -1),
    )

    next_arrays = [next_hidden]
    next_offsets = list(range(mp))
    for offset in next_offsets[1:]:
        pairs = [(device, device ^ offset) for device in range(mp)]
        next_arrays.append(lax.ppermute(next_hidden, "mp", pairs))

    early = mp // 2
    head = head_weight.reshape(head_weight.shape[0], -1)

    def early_body(*refs):
        early_kernel(next_offsets[:early], refs[:early], *refs[early:])

    total, new_hidden, new_cell = call(
        early_body,
        (jax.ShapeDtypeStruct((per_owner, head.shape[1]), F32), state, state),
        [VMEM] * (3 + early),
        *next_arrays[:early],
        next_cell,
        head,
        head_bias,
        out_specs=(VMEM, HBM, HBM),
        scratch=(pltpu.SemaphoreType.DMA((2,)),),
    )
    late = len(next_arrays) - 1

    def middle_body(*refs):
        middle_kernel(next_offsets[early:late], refs[: late - early], *refs[late - early :])

    total = call(
        middle_body,
        jax.ShapeDtypeStruct(total.shape, F32),
        [VMEM] * (2 + late - early),
        *next_arrays[early:late],
        head,
        total,
    )

    def head_body(base_ref, total_ref, *refs):
        head_kernel(
            mp, per_pair, actions, next_offsets[late:], base_ref, total_ref, refs[:1], *refs[1:]
        )

    values = call(
        head_body,
        jax.ShapeDtypeStruct((rows * lanes // 128, 1, 128), F32),
        [VMEM] * 7 + [SMEM],
        base,
        total,
        next_arrays[late],
        head,
        to_row,
        stacked,
        stacked_bias,
        value_bias,
    )
    back = lax.all_to_all(values, everyone, 0, 0, tiled=True)
    placed = call(
        functools.partial(place_kernel, mp, per_pair),
        jax.ShapeDtypeStruct((actions, capacity), F32),
        [VMEM, VMEM],
        slot,
        back,
    )
    return placed.T, new_hidden, new_cell


def solution(mesh):
    placed = (
        P("group", "mp"),
        P("group", "mp"),
        P("group", "mp"),
        P(),
        P(),
        P(None, None, "mp"),
        P(None, None, "mp"),
        P(None, "mp"),
        P(None, None, "mp"),
        P(None, "mp"),
        P("mp", None),
        P(),
        P("mp", None),
        P(),
    )
    return jax.shard_map(
        functools.partial(step, mp=mesh.shape["mp"]),
        mesh=mesh,
        in_specs=placed,
        out_specs=(P("group", None), P("group", "mp"), P("group", "mp")),
        check_vma=False,
    )
```

```python
import functools
import math

import jax
import jax.numpy as jnp
from jax import lax
from jax.experimental import pallas as pl
from jax.experimental.pallas import tpu as pltpu
from jax.sharding import PartitionSpec as P


BF16 = jnp.bfloat16
F32 = jnp.float32
I32 = jnp.int32
VMEM = pl.BlockSpec(memory_space=pltpu.VMEM)
SMEM = pl.BlockSpec(memory_space=pltpu.SMEM)
HBM = pl.BlockSpec(memory_space=pltpu.HBM)


def iota(shape, axis):
    return lax.broadcasted_iota(I32, shape, axis)


def split(values, divisor):
    if divisor & (divisor - 1) == 0:
        quotient = lax.shift_right_logical(values, jnp.int32(divisor.bit_length() - 1))
    else:
        quotient = ((values.astype(F32) + 0.5) * (1.0 / divisor)).astype(I32)
    return quotient, values - quotient * divisor


def one_hot(mask):
    return jnp.where(mask, 1.0, 0.0).astype(BF16)


def dot(left, right, contract=((1,), (0,))):
    return lax.dot_general(left, right, (contract, ((), ())), preferred_element_type=F32)


def pieces(values):
    high = values.astype(BF16)
    rest = values - high.astype(F32)
    middle = rest.astype(BF16)
    low = (rest - middle.astype(F32)).astype(BF16)
    return jnp.concatenate([high, middle, low], axis=0)


def stride_of(actions):
    return -(-(actions + 1) // 8) * 8


def span_ends(counts_ref):
    ends = []
    total = jnp.int32(0)
    for batch in range(counts_ref.shape[0]):
        total = total + counts_ref[batch]
        ends.append(total)
    return ends


def before(size):
    return one_hot(iota((size, size), 0) < iota((size, size), 1))


def route_kernel(
    mp, per_owner, counts_from, order_from, obs_from, state_from, send_to, slot_ref,
    state_ref, counts_ref, order_ref, obs_ref, send_ref, sems,
):
    copies = [
        pltpu.make_async_copy(source, held, sems.at[index])
        for index, (source, held) in enumerate(
            (
                (counts_from, counts_ref),
                (order_from, order_ref),
                (obs_from, obs_ref),
                (state_from, state_ref),
            )
        )
    ]
    for copy in copies:
        copy.start()
    blocks, capacity = order_ref.shape
    batches = counts_ref.shape[0]
    per_pair = capacity // batches
    own = lax.axis_index("group")
    lanes = iota((1, capacity), 1)
    batch_ids = iota((batches, capacity), 0)
    earlier = before(capacity)
    row_ids, rank_ids = split(iota((mp * capacity, capacity), 0), per_pair)
    row_slot = split(row_ids, mp)[0] * per_pair + rank_ids

    copies[0].wait()
    start = jnp.int32(0)
    for batch, end in enumerate(span_ends(counts_ref)):
        start = jnp.where(own == batch + 1, end, start)
    count = counts_ref[own]
    filled = lanes < count
    block, shift = split(start, capacity)
    turn = lax.rem(capacity - shift, capacity)
    copies[1].wait()
    first = order_ref[pl.ds(jnp.minimum(block, blocks - 1), 1), :]
    second = order_ref[pl.ds(jnp.minimum(block + 1, blocks - 1), 1), :]
    merged = jnp.where(lanes >= shift, first, second)
    window = pltpu.roll(jnp.broadcast_to(merged, (8, capacity)), turn, 1)[0:1]
    owner, _ = split(window, per_owner)
    by_owner = one_hot((batch_ids == owner) & filled)
    ahead = dot(by_owner, earlier)
    rank = jnp.sum(by_owner.astype(F32) * ahead, axis=0, keepdims=True).astype(I32)
    target = jnp.where(filled, owner * per_pair + rank, -1)
    copies[2].wait()
    send_ref[...] = dot(one_hot(row_slot == target), obs_ref[...]).astype(send_ref.dtype)
    out = pltpu.make_async_copy(send_ref, send_to, sems.at[4])
    out.start()
    slot_ref[0:1, :] = jnp.where(filled, owner, -1)
    slot_ref[1:2, :] = rank
    copies[3].wait()
    out.wait()


def ready_kernel(
    mp, actions, per_owner, counts_from, order_from, value_from, advantage_from, advantage_bias_from,
    hidden_from, cell_from, gate_bias_from, input_from,
    base_ref, picks_ref, to_row_ref, stacked_ref, stacked_bias_ref, hidden_ref, cell_ref, gate_bias_ref, input_ref,
    counts_ref, order_ref, value_ref, advantage_ref, advantage_bias_ref, sems,
):
    pairs = (
        (counts_from, counts_ref),
        (order_from, order_ref),
        (value_from, value_ref),
        (advantage_from, advantage_ref),
        (advantage_bias_from, advantage_bias_ref),
        (hidden_from, hidden_ref),
        (cell_from, cell_ref),
        (gate_bias_from, gate_bias_ref),
        (input_from, input_ref),
    )
    copies = [
        pltpu.make_async_copy(source, held, sems.at[index]) for index, (source, held) in enumerate(pairs)
    ]
    for copy in copies:
        copy.start()
    own = lax.axis_index("group")
    for copy in copies[:5]:
        copy.wait()

    blocks, capacity = order_ref.shape
    batches = counts_ref.shape[0]
    per_pair = capacity // batches
    ends = span_ends(counts_ref)
    lanes = iota((1, capacity), 1)
    batch_ids = iota((batches, capacity), 0)
    earlier = before(capacity)
    actors = iota((per_owner, capacity), 0) + own * per_owner
    carry = jnp.zeros((batches, 1), F32)
    base = jnp.zeros((per_owner, 1), F32)
    for index in range(blocks):
        ids = order_ref[index : index + 1, :]
        here = lanes + index * capacity
        batch = jnp.zeros((1, capacity), I32)
        for end in ends:
            batch = batch + jnp.where(here >= end, 1, 0)
        mine = (ids >= own * per_owner) & (ids < (own + 1) * per_owner)
        by_batch = one_hot((batch_ids == batch) & mine)
        ahead = dot(by_batch, earlier) + carry
        wide = by_batch.astype(F32)
        place = jnp.sum(wide * ahead, axis=0, keepdims=True)
        place = place + (batch * (mp * per_pair)).astype(F32)
        carry = carry + jnp.sum(wide, axis=1, keepdims=True)
        base = base + jnp.sum(jnp.where(ids == actors, place, 0.0), axis=1, keepdims=True)
    base = jnp.broadcast_to(base, base_ref.shape).astype(I32)
    base_ref[...] = base
    columns = iota((per_owner, picks_ref.shape[1]), 1)
    for part in range(mp):
        mask = columns == base[:, 0:1] + part * per_pair
        picks_ref[part * per_owner : (part + 1) * per_owner, :] = one_hot(mask)
    owner_rows = to_row_ref.shape[0]
    batch = split(jnp.concatenate([base] * 3, axis=0)[:, 0:1], mp * per_pair)[0]
    row_batch = split(iota((3 * per_owner, owner_rows), 1), mp)[0]
    to_row_ref[...] = jnp.where(row_batch == batch, 1.0, 0.0).T.astype(BF16)

    rows, both = stacked_ref.shape
    width = both // 2
    stride = stride_of(actions)
    row_rank, row_action = split(iota((rows, actions), 0), stride)
    pick = one_hot((row_action == iota((rows, actions), 1)) & (row_rank < per_pair))
    stacked_ref[:, width:] = dot(pick, advantage_ref[...]).astype(BF16)
    row_rank, row_action = split(iota((rows, width), 0), stride)
    value = jnp.broadcast_to(value_ref[...].astype(F32), (rows, width))
    stacked_ref[:, :width] = jnp.where((row_action <= actions) & (row_rank < per_pair), value, 0.0).astype(BF16)
    bias = advantage_bias_ref[...]
    spread = dot(pieces(jnp.broadcast_to(bias, (8, actions))), pick, ((1,), (1,)))
    stacked_bias_ref[...] = spread[0:1] + spread[8:9] + spread[16:17]
    for copy in copies[5:]:
        copy.wait()


def state_kernel(offsets, hidden_refs, state_ref, bias_ref, gates_ref):
    units = hidden_refs[0].shape[1]
    me = lax.axis_index("mp")
    gates = None
    for ref, offset in zip(hidden_refs, offsets):
        rows = pl.ds(pl.multiple_of(jnp.bitwise_xor(me, offset) * units, units), units)
        term = dot(ref[...], state_ref[rows, :])
        gates = term if gates is None else gates + term
    for k in range(4):
        columns = slice(k * units, (k + 1) * units)
        gates_ref[:, columns] = gates[:, columns] + bias_ref[k : k + 1, :]


def cell_kernel(mp, picks_ref, rows_ref, gates_ref, cell_ref, input_ref, hidden_ref, next_ref):
    per_owner, units = cell_ref.shape
    picked = dot(picks_ref[...], rows_ref[...]).astype(BF16)
    wide = [picked[part * per_owner : (part + 1) * per_owner] for part in range(mp)]
    gates = gates_ref[...] + dot(jnp.concatenate(wide, axis=1), input_ref[...])
    gate = [gates[:, k * units : (k + 1) * units] for k in range(4)]
    cell = jax.nn.sigmoid(gate[1]) * cell_ref[...].astype(F32) + jax.nn.sigmoid(gate[0]) * jnp.tanh(gate[2])
    next_ref[...] = cell.astype(BF16)
    hidden_ref[...] = (jax.nn.sigmoid(gate[3]) * jnp.tanh(cell)).astype(BF16)


def head_products(offsets, hidden_refs, head_ref):
    units = hidden_refs[0].shape[1]
    me = lax.axis_index("mp")
    total = None
    for ref, offset in zip(hidden_refs, offsets):
        rows = pl.ds(pl.multiple_of(jnp.bitwise_xor(me, offset) * units, units), units)
        term = dot(ref[...], head_ref[rows, :])
        total = term if total is None else total + term
    return total


def early_kernel(offsets, hidden_refs, cell_ref, head_ref, head_bias_ref, total_ref, hidden_to, cell_to, sems):
    copies = [
        pltpu.make_async_copy(hidden_refs[0], hidden_to, sems.at[0]),
        pltpu.make_async_copy(cell_ref, cell_to, sems.at[1]),
    ]
    for copy in copies:
        copy.start()
    bias = jnp.concatenate([head_bias_ref[0:1, :], head_bias_ref[1:2, :]], axis=1)
    total_ref[...] = head_products(offsets, hidden_refs, head_ref) + bias
    for copy in copies:
        copy.wait()


def middle_kernel(offsets, hidden_refs, head_ref, from_ref, total_ref):
    total_ref[...] = from_ref[...] + head_products(offsets, hidden_refs, head_ref)


def head_kernel(
    mp, per_pair, actions, offsets, base_ref, total_ref, hidden_refs, head_ref, to_row_ref, stacked_ref,
    stacked_bias_ref, value_bias_ref, send_ref,
):
    total = total_ref[...] + head_products(offsets, hidden_refs, head_ref)
    streams = jnp.maximum(total, 0.0).astype(BF16)
    spread = dot(streams, stacked_ref[...], ((1,), (1,)))
    first = jnp.where(lax.axis_index("mp") == 0, 1.0, 0.0)
    spread = spread + (stacked_bias_ref[...] + value_bias_ref[0]) * first
    _, rank = split(base_ref[:, 0:1], mp * per_pair)
    lane_rank, _ = split(iota((1, spread.shape[1]), 1), stride_of(actions))
    spread = jnp.where(lane_rank == rank, spread, 0.0)
    out = dot(to_row_ref[...], pieces(spread))
    chunks = out.shape[1] // 128
    for chunk in range(chunks):
        send_ref[pl.ds(chunk, out.shape[0], chunks), 0, :] = out[:, chunk * 128 : (chunk + 1) * 128]


def place_kernel(mp, per_pair, slot_ref, rows_ref, out_ref):
    actions, capacity = out_ref.shape
    stride = stride_of(actions)
    chunks = -(-per_pair * stride // 128)
    owners = rows_ref.shape[0] // (mp * chunks)
    owner = slot_ref[0:1, :]
    rank = slot_ref[1:2, :]
    columns = []
    for chunk in range(chunks):
        total = rows_ref[pl.ds(chunk, owners, mp * chunks), 0, :]
        for part in range(1, mp):
            total = total + rows_ref[pl.ds(part * chunks + chunk, owners, mp * chunks), 0, :]
        columns.append(total)
    to_slot = one_hot(iota((owners, capacity), 0) == owner)
    to_slot = jnp.concatenate([to_slot] * 3, axis=0)
    spread = dot(pieces(jnp.concatenate(columns, axis=1)), to_slot, ((0,), (0,)))
    total = jnp.zeros((stride, capacity), F32)
    for index in range(per_pair):
        total = total + jnp.where(rank == index, spread[index * stride : (index + 1) * stride, :], 0.0)
    row = iota((stride, capacity), 0)
    weights = jnp.where(row < actions, 1.0 / actions, jnp.where(row == actions, -1.0, 0.0))
    total = total - jnp.sum(total * weights, axis=0, keepdims=True)
    out_ref[...] = total[:actions, :]


def in_hbm(array):
    return pltpu.with_memory_space_constraint(array, pltpu.HBM)


def call(kernel, out_shape, specs, *args, out_specs=None, scratch=()):
    held = [math.prod(x.shape) * x.dtype.itemsize for x in (*args, *jax.tree.leaves(out_shape))]
    return pl.pallas_call(
        kernel,
        out_shape=out_shape,
        in_specs=specs,
        out_specs=out_specs or jax.tree.map(lambda _: VMEM, out_shape),
        scratch_shapes=list(scratch),
        compiler_params=pltpu.CompilerParams(vmem_limit_bytes=2 * sum(held) + (4 << 20)),
    )(*args)


def gather_parts(part, mp):
    arrays = [part]
    offsets = [0]
    distance = mp // 2
    while distance:
        pairs = [(device, device ^ distance) for device in range(mp)]
        got = []
        for array in arrays:
            got.append(lax.ppermute(array, "mp", pairs))
        arrays += got
        offsets += [offset ^ distance for offset in offsets]
        distance //= 2
    return arrays, offsets


def step(
    observations,
    hidden_state,
    cell_state,
    arrival_order,
    batch_counts,
    input_weight,
    state_weight,
    gate_bias,
    head_weight,
    head_bias,
    value_weight,
    value_bias,
    advantage_weight,
    advantage_bias,
    *,
    mp,
):
    batches = batch_counts.shape[0]
    capacity, features = observations.shape
    per_owner, units = cell_state.shape
    per_pair = capacity // batches
    actions = advantage_weight.shape[1]
    rows = batches * mp
    everyone = ("group", "mp")

    stride = stride_of(actions)
    lanes = -(-per_pair * stride // 128) * 128
    order = arrival_order.reshape(-1, capacity)

    hidden_arrays, offsets = gather_parts(hidden_state, mp)
    send, slot, state_held = call(
        functools.partial(route_kernel, mp, per_owner),
        (
            jax.ShapeDtypeStruct((rows * per_pair, features), BF16),
            jax.ShapeDtypeStruct((2, capacity), I32),
            jax.ShapeDtypeStruct(state_weight.shape, BF16),
        ),
        [HBM, HBM, HBM, HBM],
        *map(in_hbm, (batch_counts, order, observations, state_weight)),
        out_specs=(HBM, VMEM, VMEM),
        scratch=(
            pltpu.SMEM(batch_counts.shape, I32),
            pltpu.VMEM(order.shape, I32),
            pltpu.VMEM(observations.shape, BF16),
            pltpu.VMEM((rows * per_pair, features), BF16),
            pltpu.SemaphoreType.DMA((5,)),
        ),
    )
    got = lax.all_to_all(send, everyone, 0, 0, tiled=True)

    sources = (
        batch_counts,
        order,
        value_weight.T,
        advantage_weight.T,
        advantage_bias.reshape(1, -1),
        hidden_state,
        cell_state,
        gate_bias,
        input_weight,
    )
    base, picks, to_row, stacked, stacked_bias, hidden_held, cell_held, gate_bias_held, input_held = call(
        functools.partial(ready_kernel, mp, actions, per_owner),
        (
            jax.ShapeDtypeStruct((per_owner, 128), I32),
            jax.ShapeDtypeStruct((mp * per_owner, rows * per_pair), BF16),
            jax.ShapeDtypeStruct((rows, 3 * per_owner), BF16),
            jax.ShapeDtypeStruct((lanes, 2 * head_bias.shape[1]), BF16),
            jax.ShapeDtypeStruct((1, lanes), F32),
            *(jax.ShapeDtypeStruct(x.shape, x.dtype) for x in sources[5:]),
        ),
        [HBM] * len(sources),
        *map(in_hbm, sources),
        scratch=(
            pltpu.SMEM(batch_counts.shape, I32),
            *(pltpu.VMEM(x.shape, x.dtype) for x in sources[1:5]),
            pltpu.SemaphoreType.DMA((len(sources),)),
        ),
    )
    count = len(hidden_arrays)

    def state_body(*refs):
        state_kernel(offsets, refs[:count], *refs[count:])

    gates = call(
        state_body,
        jax.ShapeDtypeStruct((per_owner, 4 * units), F32),
        [VMEM] * (2 + count),
        hidden_held,
        *hidden_arrays[1:],
        state_held.reshape(state_held.shape[0], -1),
        gate_bias_held,
    )

    state = jax.ShapeDtypeStruct((per_owner, units), BF16)
    next_hidden, next_cell = call(
        functools.partial(cell_kernel, mp),
        (state, state),
        [VMEM] * 5,
        picks,
        got,
        gates,
        cell_held,
        input_held.reshape(input_held.shape[0], -1),
    )

    next_arrays = [next_hidden]
    next_offsets = list(range(mp))
    for offset in next_offsets[1:]:
        pairs = [(device, device ^ offset) for device in range(mp)]
        next_arrays.append(lax.ppermute(next_hidden, "mp", pairs))

    early = mp // 2
    head = head_weight.reshape(head_weight.shape[0], -1)

    def early_body(*refs):
        early_kernel(next_offsets[:early], refs[:early], *refs[early:])

    total, new_hidden, new_cell = call(
        early_body,
        (jax.ShapeDtypeStruct((per_owner, head.shape[1]), F32), state, state),
        [VMEM] * (3 + early),
        *next_arrays[:early],
        next_cell,
        head,
        head_bias,
        out_specs=(VMEM, HBM, HBM),
        scratch=(pltpu.SemaphoreType.DMA((2,)),),
    )
    late = len(next_arrays) - 1

    def middle_body(*refs):
        middle_kernel(next_offsets[early:late], refs[: late - early], *refs[late - early :])

    total = call(
        middle_body,
        jax.ShapeDtypeStruct(total.shape, F32),
        [VMEM] * (2 + late - early),
        *next_arrays[early:late],
        head,
        total,
    )

    def head_body(base_ref, total_ref, *refs):
        head_kernel(
            mp, per_pair, actions, next_offsets[late:], base_ref, total_ref, refs[:1], *refs[1:]
        )

    values = call(
        head_body,
        jax.ShapeDtypeStruct((rows * lanes // 128, 1, 128), F32),
        [VMEM] * 7 + [SMEM],
        base,
        total,
        next_arrays[late],
        head,
        to_row,
        stacked,
        stacked_bias,
        value_bias,
    )
    back = lax.all_to_all(values, everyone, 0, 0, tiled=True)
    placed = call(
        functools.partial(place_kernel, mp, per_pair),
        jax.ShapeDtypeStruct((actions, capacity), F32),
        [VMEM, VMEM],
        slot,
        back,
    )
    return placed.T, new_hidden, new_cell


def solution(mesh):
    placed = (
        P("group", "mp"),
        P("group", "mp"),
        P("group", "mp"),
        P(),
        P(),
        P(None, None, "mp"),
        P(None, None, "mp"),
        P(None, "mp"),
        P(None, None, "mp"),
        P(None, "mp"),
        P("mp", None),
        P(),
        P("mp", None),
        P(),
    )
    return jax.shard_map(
        functools.partial(step, mp=mesh.shape["mp"]),
        mesh=mesh,
        in_specs=placed,
        out_specs=(P("group", None), P("group", "mp"), P("group", "mp")),
        check_vma=False,
    )
```
